32 devices in a mesh: group: 2 (over x), tensor: 16 (over z, y, core).
Axes of the slice: x: 2, y: 2, z: 4, core: 2. Of those that a mesh axis runs over, the one named last changes fastest.
Arguments:
- hidden_in: bfloat16 [256, 2048], P(('group', 'tensor')), parts along dimension 0, may hold values from -6 to 6
- queries: bfloat16 [1024, 2048], P(('group', 'tensor')), parts along dimension 0, may hold values from -6 to 6
- kv_cache: bfloat16 [1024, 64, 256], P(('group', 'tensor')), parts along dimension 0, may hold values from -6 to 6
- new_kv: bfloat16 [1024, 256], P(('group', 'tensor')), parts along dimension 0, may hold values from -8 to 8
- cycle_pos: int32 [256], P('group'), parts along dimension 0, may hold values from 0 to 59
- out_weight: bfloat16 [8192, 2048], P('tensor'), may hold values from -0.125 to 0.125
- norm_gain: float32 [2048], replicated, may hold values from 0.1 to 1.9
- route_logits: float32 [256, 8], P(('group', 'tensor')), parts along dimension 0, may hold values from -6 to 303
- expert_ids: int32 [256, 8], P(('group', 'tensor')), parts along dimension 0, may hold values from 0 to 15, all different within a row; in each aligned block of 8 rows (0 to 7, 8 to 15, ...) at most 8 rows name the same one
- expert_in: bfloat16 [16, 2048, 1536], P('tensor'), may hold values from -0.125 to 0.125
- expert_out: bfloat16 [16, 768, 2048], P('tensor'), may hold values from -0.21875 to 0.21875
Outputs:
- hidden_out: bfloat16 [256, 2048], P(('group', 'tensor')), parts along dimension 0
- new_cache: bfloat16 [1024, 64, 256], P(('group', 'tensor')), parts along dimension 0
The draws below stay inside these ranges and needn't reach their ends.
There are 2 independent parts, one for each index of `group`. The reference program is written for one: setup_inputs(seed, part) draws one part's arguments, and reference() takes and returns one part's arrays. A program takes and returns all parts, laid end to end along the dimension named above; an argument that names none is the same for every part. Nothing has to cross between parts.
Inputs may be any that keep to these rules, and one draw needn't show every extreme that they name: `expert_ids`: among the rows of one device no expert is named more than 8 times, a bound that some block reaches there in some device's rows. The 8 experts of a row differ.
All inputs are finite; a program needn't handle non-finite values.
Results may differ from the reference program's by a relative error of at most 0.0063.
Values may be sent and summed in bfloat16 or wider, within the bound.
A program may use at most 64 MiB of HBM per device.

```python
import math
import jax
import jax.numpy as jnp
import numpy as np
from jax import lax

D = 2048
FF = 768
HD = 128
KVH = 4
HQ = 64
TOP = 8
SINK = 4
WIN = 60
STR_DEV = 8
STREAMS = 128
EXPERTS = 16
G = 16
SLOTS = 64
CAP = 8
N_TENSOR = 16


def draw_queries(key, part):
    own_key = jax.random.fold_in(key, 3)
    row_count = KVH * STREAMS
    backdrop = jnp.clip(jax.random.normal(own_key, (row_count, G * HD)), -6.0, 6.0)
    return backdrop.astype(jnp.bfloat16)


def draw_kv_cache(key, part):
    own_key = jax.random.fold_in(key, 5)
    row_count = KVH * STREAMS
    backdrop = jnp.clip(jax.random.normal(own_key, (row_count, SLOTS, 2 * HD)), -6.0, 6.0)
    return backdrop.astype(jnp.bfloat16)


def draw_route_logits(key, part):
    own_key = jax.random.fold_in(key, 7)
    key_base = jax.random.fold_in(own_key, 0)
    return jnp.clip(1.5 * jax.random.normal(key_base, (STREAMS, TOP)), -6.0, 6.0).astype(jnp.float32)


def draw_hidden_in(key, part):
    own_key = jax.random.fold_in(key, 9)
    key_base = jax.random.fold_in(own_key, 0)
    backdrop = jax.random.normal(key_base, (STREAMS, D))
    return jnp.clip(0.7 * backdrop, -6.0, 6.0).astype(jnp.bfloat16)


def place_ends(array, key, least, top_value):
    longest = array.shape.index(max(array.shape))
    spots = []
    for shift in (0, 1):
        where = [jax.random.randint(jax.random.fold_in(key, axis), (), 0, length) for axis, length in enumerate(array.shape)]
        where[longest] = (where[longest] + shift) % array.shape[longest]
        spots.append(tuple(where))
    return array.at[spots[0]].set(least).at[spots[1]].set(top_value)


def levels(stream_key, extent, pieces, least, high):
    def one(axis_at, blocks):
        steps = jax.random.uniform(jax.random.fold_in(jax.random.fold_in(stream_key, 6), axis_at), (blocks,), jnp.float32, least / len(pieces), high / len(pieces))
        return jnp.repeat(jnp.exp(steps), extent[axis_at] // blocks).reshape((-1,) + (1,) * (len(extent) - axis_at - 1))

    gain = one(*pieces[0])
    for cut in pieces[1:]:
        gain = gain * one(*cut)
    return gain


def assign_block(rng, own, number, rows, number_of, top, bound, skew):
    sequence = jax.random.permutation(rng, number_of)
    heavy_load, ordinary = shares(number_of, rows * top, bound, skew, True), shares(number_of, rows * top, bound, skew, False)
    places = jnp.arange(number_of)

    def named(lengths, turn):
        used = int((lengths > 0).sum())
        fixed = max(1, used // 4)
        shifted = fixed + (places - fixed + turn * (used - fixed)) % max(1, number_of - fixed)
        return jnp.zeros((number_of,), jnp.int32).at[sequence[jnp.where(places < fixed, places, shifted)]].set(jnp.asarray(lengths, jnp.int32))

    lengths = jnp.where(number % 4 == 0, named(heavy_load, number // 4), named(ordinary, number - number // 4 - 1))
    mixed = jax.random.permutation(jax.random.fold_in(own, 3), number_of)
    giver, sink = mixed[0:number_of // 2 * 2:2], mixed[1:number_of // 2 * 2:2]
    slack = jnp.minimum(lengths[giver] - 1, bound - lengths[sink]) // 2
    slack = jnp.where((giver == sequence[0]) | (sink == sequence[0]) | (lengths[sink] == 0), 0, jnp.maximum(slack, 0))
    shifted = jax.random.randint(jax.random.fold_in(own, 4), (number_of // 2,), 0, 1 << 20) % (slack + 1)
    lengths = lengths.at[giver].add(-shifted).at[sink].add(shifted)
    items = jnp.searchsorted(jnp.cumsum(lengths), jnp.arange(rows * top), side="right").astype(jnp.int32)
    grid = items.reshape(top, rows).T
    grid = grid[jax.random.permutation(jax.random.fold_in(own, 1), rows)]
    turn = jax.random.randint(jax.random.fold_in(own, 2), (rows, 1), 0, top)
    return jnp.take_along_axis(grid, (jnp.arange(top)[None, :] + turn) % top, axis=1)


def shares(number_of, total, limit, lean, full):
    loads = [(1 << 20) // math.isqrt(standing ** lean) + 1 for standing in range(1, number_of + 1)]
    largest = limit if full else min(limit, max(-(-total // number_of), total * loads[0] // sum(loads)))
    least = 1 if total - largest >= number_of - 1 else 0
    holding, surplus = [largest] + [least] * (number_of - 1), total - largest - least * (number_of - 1)
    while surplus > 0:
        free = [i for i in range(1, number_of) if holding[i] < largest] or [i for i in range(1, number_of) if holding[i] < limit]
        whole, budget = sum([loads[i] for i in free]), surplus
        for i in free:
            addition = min(limit - holding[i], max(1, budget * loads[i] // whole), surplus)
            holding[i] = holding[i] + addition
            surplus = surplus - addition
    return np.array(holding)


def gaussian(key, dims, spread, limit, cuts=(), held_as=jnp.bfloat16):
    drawn = spread * jax.random.normal(key, dims, jnp.float32)
    if cuts:
        drawn = drawn * levels(key, dims, cuts, -0.22, 0.18)
    return jnp.clip(drawn, -limit, limit).astype(held_as)


def setup_inputs(seed: int = 0, part: int = 0) -> dict:
    seeds = jax.random.split(jax.random.key(seed), 12)
    part_keys = jax.random.split(jax.random.fold_in(seeds[11], part), 12)
    hidden_in = draw_hidden_in(jax.random.fold_in(jax.random.fold_in(seeds[11], part), 71), part)
    queries = draw_queries(jax.random.fold_in(jax.random.fold_in(seeds[11], part), 71), part)
    kv_cache = draw_kv_cache(jax.random.fold_in(jax.random.fold_in(seeds[11], part), 71), part)
    new_kv = gaussian(part_keys[3], (KVH * STREAMS, 2 * HD), 2.0, 8.0, ((0, 16),))
    cycle_pos = place_ends(jax.random.randint(part_keys[4], (STREAMS,), 0, WIN), jax.random.fold_in(part_keys[4], 1), 0, WIN - 1).astype(jnp.int32)
    out_weight = gaussian(seeds[5], (HQ * HD, D), (HQ * HD // 4) ** -0.5, 0.125, ((0, 16),))
    norm_gain = jnp.clip(1.0 + 0.18 * jax.random.normal(seeds[6], (D,), jnp.float32), 0.1, 1.9)
    route_logits = draw_route_logits(jax.random.fold_in(jax.random.fold_in(seeds[11], part), 71), part)
    expert_ids_keys = jax.random.split(jax.random.fold_in(part_keys[8], 1), STREAMS // STR_DEV)
    expert_ids_turns = jax.random.permutation(jax.random.fold_in(part_keys[8], 3), STREAMS // STR_DEV)
    expert_ids = jax.vmap(lambda own, number: assign_block(jax.random.fold_in(part_keys[8], 2), own, number, STR_DEV, EXPERTS, TOP, CAP, 3))(expert_ids_keys, expert_ids_turns).reshape((STREAMS, TOP))
    expert_in = gaussian(seeds[9], (EXPERTS, D, 2 * FF), D ** -0.5, 0.125, ((0, 16),))
    expert_out = gaussian(seeds[10], (EXPERTS, FF, D), FF ** -0.5, 0.21875, ((0, 16),))
    return {"hidden_in": hidden_in, "queries": queries, "kv_cache": kv_cache, "new_kv": new_kv, "cycle_pos": cycle_pos, "out_weight": out_weight, "norm_gain": norm_gain, "route_logits": route_logits, "expert_ids": expert_ids, "expert_in": expert_in, "expert_out": expert_out}


def reference(hidden_in, queries, kv_cache, new_kv, cycle_pos, out_weight, norm_gain, route_logits, expert_ids, expert_in, expert_out):
    row_count = KVH * STREAMS
    slot_index = (jnp.repeat(cycle_pos, KVH) + SINK).astype(jnp.int32)
    write_mask = lax.broadcasted_iota(jnp.int32, (row_count, SLOTS), 1) == slot_index[:, None]
    new_cache = jnp.where(write_mask[:, :, None], new_kv[:, None, :], kv_cache)
    key_part = new_cache[:, :, :HD].astype(jnp.float32)
    value_part = new_cache[:, :, HD:].astype(jnp.float32)
    query_heads = queries.reshape(row_count, G, HD).astype(jnp.float32)
    scores = jnp.einsum('rhk,rsk->rhs', query_heads, key_part) / math.sqrt(HD)
    peak = lax.optimization_barrier(jnp.max(scores, axis=-1, keepdims=True))
    weights = jnp.exp(scores - peak)
    attn_probs = (weights / lax.optimization_barrier(jnp.sum(weights, axis=-1, keepdims=True))).astype(jnp.bfloat16)
    head_out = jnp.einsum('rhs,rsk->rhk', attn_probs.astype(jnp.float32), value_part).astype(jnp.bfloat16)
    attention = head_out.reshape(STREAMS, HQ * HD)
    attn_proj = jnp.dot(attention, out_weight, preferred_element_type=jnp.float32)
    mid_state = (hidden_in.astype(jnp.float32) + attn_proj).astype(jnp.bfloat16)
    mid_wide = mid_state.astype(jnp.float32)
    normed = (mid_wide * lax.rsqrt(lax.optimization_barrier(jnp.mean(mid_wide * mid_wide, axis=-1, keepdims=True)) + 1e-06) * norm_gain).astype(jnp.bfloat16)
    gate_probs = jax.nn.softmax(route_logits.astype(jnp.float32), axis=-1).astype(jnp.bfloat16)
    slot_count = N_TENSOR * CAP

    def one_expert(moe_total, expert):
        matches = expert_ids == expert
        chosen = jnp.any(matches, axis=1)
        weight_tok = lax.optimization_barrier(jnp.sum(jnp.where(matches, gate_probs.astype(jnp.float32), jnp.float32(0.0)), axis=1))
        picked_rows = jnp.nonzero(chosen, size=slot_count, fill_value=0)[0].astype(jnp.int32)
        filled = jnp.arange(slot_count, dtype=jnp.int32) < jnp.sum(chosen.astype(jnp.int32))
        rows_in = normed[picked_rows]
        joined = jnp.dot(rows_in, expert_in[expert], preferred_element_type=jnp.float32)
        activated = (jax.nn.silu(joined[:, :FF]) * joined[:, FF:]).astype(jnp.bfloat16)
        result = jnp.dot(activated, expert_out[expert], preferred_element_type=jnp.float32).astype(jnp.bfloat16)
        factor = jnp.where(filled, weight_tok[picked_rows], jnp.float32(0.0))
        moe_total = moe_total.at[picked_rows].add(factor[:, None] * result.astype(jnp.float32))
        return (moe_total, None)
    moe_total, _ = lax.scan(one_expert, jnp.zeros((STREAMS, D), jnp.float32), jnp.arange(EXPERTS, dtype=jnp.int32))
    hidden_out = (mid_state.astype(jnp.float32) + moe_total).astype(jnp.bfloat16)
    return (hidden_out, new_cache)
```

```python
import functools
import math

import jax
import jax.numpy as jnp
from jax import lax
from jax.experimental import pallas as pl
from jax.experimental.pallas import tpu as pltpu
from jax.sharding import PartitionSpec as P

HD = 128
SINK = 4
MESH = pl.DeviceIdType.MESH


def wait_bytes(ref, sem):
    pltpu.make_async_copy(ref, ref, sem).wait()


CHUNKS = 4


def layer_kernel(
    n,
    queries_hbm,
    hidden_hbm,
    gain_hbm,
    logits_hbm,
    ids_hbm,
    new_kv_hbm,
    cycle_hbm,
    kv_cache,
    out_weight,
    expert_in,
    expert_out,
    hidden_out,
    cache,
    queries,
    hidden_in,
    norm_gain,
    route_logits,
    expert_ids,
    new_kv,
    cycle_pos,
    w_proj,
    w_in,
    w_out,
    query_rows,
    score_rows,
    out_rows,
    by_head,
    heads,
    core_out,
    core_in,
    mine,
    chip_out,
    chip_in,
    mid,
    gathered,
    gathered_last,
    joined,
    act,
    load_sem,
    head_send,
    head_recv,
    core_send,
    core_recv,
    chip_send,
    chip_recv,
    ag_send,
    ag_recv,
    relay_send,
    relay_recv,
):
    me = lax.axis_index("tensor")
    chips = n // 2
    chip, core = me // 2, me % 2
    partner = chip * 2 + (1 - core)
    tokens, width = hidden_in.shape
    ff = w_out.shape[0]
    half = chips * tokens
    part = width // CHUNKS
    f32, bf16 = jnp.float32, jnp.bfloat16

    barrier = pltpu.get_barrier_semaphore()

    @pl.loop(1, n)
    def _(k):
        pl.semaphore_signal(
            barrier, inc=1, device_id={"tensor": lax.rem(me + k, n)}, device_id_type=MESH
        )

    pairs = (
        (kv_cache, cache),
        (queries_hbm, queries),
        (new_kv_hbm, new_kv),
        (cycle_hbm, cycle_pos),
        (logits_hbm, route_logits),
        (ids_hbm, expert_ids),
        (hidden_hbm, hidden_in),
        (gain_hbm, norm_gain),
        (out_weight, w_proj),
        (expert_in.at[0], w_in),
        (expert_out.at[0], w_out),
    )
    loads = [pltpu.make_async_copy(a, b, load_sem.at[i]) for i, (a, b) in enumerate(pairs)]
    for load in loads[:8]:
        load.start()

    rows_here = cache.shape[0]
    kv_heads = rows_here // tokens
    per_kv = queries.shape[1] // HD
    loads[1].wait()
    for h in range(per_kv):
        query_rows[h * rows_here : (h + 1) * rows_here, :] = queries[
            :, h * HD : (h + 1) * HD
        ].astype(f32)
    for load in (loads[0], loads[2], loads[3]):
        load.wait()
    for load in loads[8:]:
        load.start()
    slot_ids = lax.broadcasted_iota(jnp.int32, cache.shape[1:], 0)
    for t in range(tokens):
        written = slot_ids == cycle_pos[me * tokens + t] + SINK
        for r in range(t * kv_heads, (t + 1) * kv_heads):
            cache[r] = jnp.where(
                written, new_kv[r : r + 1, :].astype(f32), cache[r].astype(f32)
            ).astype(bf16)
    for r in range(rows_here):
        query = query_rows[pl.ds(r, per_kv, stride=rows_here), :].astype(bf16)
        score_rows[r * per_kv : (r + 1) * per_kv, :] = lax.dot_general(
            query,
            cache[r, :, :HD],
            (((1,), (1,)), ((), ())),
            preferred_element_type=f32,
        )
    scores = score_rows[...] / math.sqrt(HD)
    powers = jnp.exp(scores - jnp.max(scores, axis=-1, keepdims=True))
    score_rows[...] = powers / jnp.sum(powers, axis=-1, keepdims=True)
    for r in range(rows_here):
        probs = score_rows[r * per_kv : (r + 1) * per_kv, :].astype(bf16)
        first = (r % kv_heads) * per_kv * tokens + r // kv_heads
        out_rows[pl.ds(first, per_kv, stride=tokens), :] = jnp.dot(
            probs, cache[r, :, HD:], preferred_element_type=f32
        )
    by_head[...] = out_rows[...].reshape(by_head.shape).astype(bf16)

    pl.semaphore_wait(barrier, n - 1)

    def slot(device):
        return lax.rem(device, 2) * chips + device // 2

    my_slot = slot(me)

    @pl.loop(1, n)
    def _(k):
        to = lax.rem(me + k, n)
        pltpu.make_async_remote_copy(
            src_ref=by_head.at[to],
            dst_ref=heads.at[my_slot],
            send_sem=head_send,
            recv_sem=head_recv,
            device_id={"tensor": to},
            device_id_type=MESH,
        ).start()

    heads[my_slot] = by_head[me]

    for load in loads[4:8]:
        load.wait()
    logits = route_logits[...]
    top = logits.shape[1]
    powers = jnp.exp(logits - jnp.max(logits, axis=-1, keepdims=True))
    gate = (powers / jnp.sum(powers, axis=-1, keepdims=True)).astype(bf16).astype(f32)
    pad = gathered_last.shape[2] - part
    lanes = lax.broadcasted_iota(jnp.int32, (tokens, pad), 1)
    ids = expert_ids[...]
    table = jnp.zeros((tokens, pad), f32)
    for j in range(top):
        table = table + jnp.where(lanes == ids[:, j : j + 1], gate[:, j : j + 1], 0.0)

    def block(c):
        return gathered_last if c == CHUNKS - 1 else gathered.at[c]

    def rows_of(ref, lo, hi):
        other = ref[pl.ds((1 - core) * chips, chips), :, lo:hi].astype(f32)
        own = ref[pl.ds(core * chips, chips), :, lo:hi].astype(f32)
        return jnp.concatenate(
            [other.reshape(half, hi - lo), own.reshape(half, hi - lo)], axis=0
        )

    def head_rows(parity):
        rows = heads[pl.ds(parity * chips, chips)].astype(f32)
        return jnp.concatenate(
            [rows[:, h].reshape(half, HD) for h in range(heads.shape[1])], axis=-1
        ).astype(bf16)

    def core_copy(r, c):
        return pltpu.make_async_remote_copy(
            src_ref=core_out.at[r, c],
            dst_ref=core_in.at[r, c],
            send_sem=core_send.at[r, c],
            recv_sem=core_recv.at[r, c],
            device_id={"tensor": partner},
            device_id_type=MESH,
        )

    def exchange(r, c, rows):
        core_out[r, c] = rows[:half].reshape(chips, tokens, part).astype(bf16)
        core_copy(r, c).start()
        mine[c] = rows[half:].reshape(chips, tokens, part)

    def scatter(r, c):
        core_copy(r, c).wait_recv()
        chip_out[r, c] = (mine[c] + core_in[r, c].astype(f32)).astype(bf16)

        @pl.loop(1, chips)
        def _(step):
            to = lax.rem(chip + step, chips)
            pltpu.make_async_remote_copy(
                src_ref=chip_out.at[r, c, to],
                dst_ref=chip_in.at[r, c, chip],
                send_sem=chip_send.at[r, c],
                recv_sem=chip_recv.at[r, c],
                device_id={"tensor": to * 2 + core},
                device_id_type=MESH,
            ).start()

        chip_in[r, c, chip] = chip_out[r, c, chip]

    def collect(r, c):
        wait_bytes(chip_in.at[r, c, pl.ds(0, chips - 1)], chip_recv.at[r, c])
        return jnp.sum(chip_in[r, c].astype(f32), axis=0)

    wait_bytes(heads.at[pl.ds(0, n - 1)], head_recv)
    loads[8].wait()
    head_all = jnp.concatenate([head_rows(1 - core), head_rows(core)], axis=0)
    for c in range(CHUNKS):
        exchange(
            0,
            c,
            jnp.dot(head_all, w_proj[:, c * part : (c + 1) * part], preferred_element_type=f32),
        )
    for c in range(CHUNKS):
        scatter(0, c)

    squares = jnp.zeros((tokens, 1), f32)
    for c in range(CHUNKS):
        columns = slice(c * part, (c + 1) * part)
        wide = (hidden_in[:, columns].astype(f32) + collect(0, c)).astype(bf16).astype(f32)
        mid[:, columns] = wide
        squares = squares + jnp.sum(wide * wide, axis=-1, keepdims=True)
        to_send = block(c)
        to_send[my_slot, :, :part] = (wide * norm_gain[:, columns]).astype(bf16)
        if c == CHUNKS - 1:
            scale = lax.rsqrt(squares / width + 1e-06)
            high = scale.astype(bf16).astype(f32)
            info = jnp.where(lanes == n, high, jnp.where(lanes == n + 1, scale - high, table))
            to_send[my_slot, :, part:] = info.astype(bf16)

        @pl.loop(1, chips)
        def _(step, c=c, to_send=to_send):
            to = lax.rem(chip + step, chips)
            pltpu.make_async_remote_copy(
                src_ref=to_send.at[my_slot],
                dst_ref=to_send.at[my_slot],
                send_sem=ag_send.at[c],
                recv_sem=ag_recv.at[c],
                device_id={"tensor": to * 2 + core},
                device_id_type=MESH,
            ).start()

    def relay(c):
        rows = block(c).at[pl.ds(core * chips, chips)]
        return pltpu.make_async_remote_copy(
            src_ref=rows,
            dst_ref=rows,
            send_sem=relay_send.at[c],
            recv_sem=relay_recv.at[c],
            device_id={"tensor": partner},
            device_id_type=MESH,
        )

    piece = 256

    def product(rows, c, lo):
        term = jnp.dot(
            rows,
            w_in[c * part : (c + 1) * part, lo : lo + piece],
            preferred_element_type=f32,
        )
        return term if c == 0 else joined[:, lo : lo + piece] + term

    for c in range(CHUNKS):
        wait_bytes(block(c).at[pl.ds(0, chips - 1)], ag_recv.at[c])
        relay(c).start()
        if c == 0:
            loads[9].wait()
            continue
        wait_bytes(block(c - 1).at[pl.ds(0, chips)], relay_recv.at[c - 1])
        rows = rows_of(block(c - 1), 0, part).astype(bf16)
        for lo in range(0, 2 * ff, piece):
            joined[:, lo : lo + piece] = product(rows, c - 1, lo)
    last = CHUNKS - 1
    loads[10].wait()
    wait_bytes(block(last).at[pl.ds(0, chips)], relay_recv.at[last])
    lane = lax.broadcasted_iota(jnp.int32, (2 * half, pad), 1)
    info = rows_of(block(last), part, part + pad)
    share = jnp.sum(jnp.where(lane == me, info, 0.0), axis=-1, keepdims=True)
    scale = jnp.sum(
        jnp.where((lane == n) | (lane == n + 1), info, 0.0), axis=-1, keepdims=True
    )
    rows = rows_of(block(last), 0, part).astype(bf16)
    for lo in range(0, ff, piece):
        gate_part = product(rows, last, lo) * scale
        up_part = product(rows, last, ff + lo) * scale
        act[:, lo : lo + piece] = (gate_part / (1.0 + jnp.exp(-gate_part)) * up_part).astype(bf16)

    for c in range(CHUNKS):
        result = jnp.dot(
            act[...], w_out[:, c * part : (c + 1) * part], preferred_element_type=f32
        )
        exchange(1, c, result.astype(bf16).astype(f32) * share)
    for c in range(CHUNKS):
        scatter(1, c)
    for c in range(CHUNKS):
        columns = slice(c * part, (c + 1) * part)
        hidden_out[:, columns] = (mid[:, columns] + collect(1, c)).astype(bf16)

    wait_bytes(heads.at[pl.ds(0, n - 1)], head_send)
    for c in range(CHUNKS):
        for r in range(2):
            core_copy(r, c).wait_send()
            wait_bytes(chip_out.at[r, c, pl.ds(0, chips - 1)], chip_send.at[r, c])
        wait_bytes(block(c).at[pl.ds(0, chips - 1)], ag_send.at[c])
        relay(c).wait_send()


def layer(n, queries, hidden_in, norm_gain, route_logits, expert_ids, new_kv, cycle_pos, kv_cache, weights):
    tokens, width = hidden_in.shape
    out_weight, expert_in, expert_out = weights
    ff = expert_out.shape[1]
    chips = n // 2
    part = width // CHUNKS
    pad = -(-(n + 2) // 128) * 128
    rows_here, slots, _ = kv_cache.shape
    heads_all = rows_here // tokens * (queries.shape[1] // HD)
    exchange = (n, heads_all // n, tokens, HD)
    bf16, f32 = jnp.bfloat16, jnp.float32
    hbm = pl.BlockSpec(memory_space=pl.ANY)
    vmem = pl.BlockSpec(memory_space=pltpu.VMEM)
    dma = pltpu.SemaphoreType.DMA
    small = (queries, hidden_in, norm_gain, route_logits, expert_ids, new_kv)
    return pl.pallas_call(
        functools.partial(layer_kernel, n),
        out_shape=(
            pltpu.VMEM((tokens, width), bf16),
            pltpu.VMEM(kv_cache.shape, bf16),
        ),
        in_specs=[hbm] * 11,
        out_specs=(vmem, vmem),
        scratch_shapes=[pltpu.VMEM(a.shape, a.dtype) for a in small]
        + [
            pltpu.SMEM(cycle_pos.shape, cycle_pos.dtype),
            pltpu.VMEM(out_weight.shape, bf16),
            pltpu.VMEM(expert_in.shape[1:], bf16),
            pltpu.VMEM(expert_out.shape[1:], bf16),
            pltpu.VMEM((heads_all * tokens, HD), f32),
            pltpu.VMEM((heads_all * tokens, slots), f32),
            pltpu.VMEM((heads_all * tokens, HD), f32),
            pltpu.VMEM(exchange, bf16),
            pltpu.VMEM(exchange, bf16),
            pltpu.VMEM((2, CHUNKS, chips, tokens, part), bf16),
            pltpu.VMEM((2, CHUNKS, chips, tokens, part), bf16),
            pltpu.VMEM((CHUNKS, chips, tokens, part), f32),
            pltpu.VMEM((2, CHUNKS, chips, tokens, part), bf16),
            pltpu.VMEM((2, CHUNKS, chips, tokens, part), bf16),
            pltpu.VMEM((tokens, width), f32),
            pltpu.VMEM((CHUNKS - 1, n, tokens, part), bf16),
            pltpu.VMEM((n, tokens, part + pad), bf16),
            pltpu.VMEM((n * tokens, 2 * ff), f32),
            pltpu.VMEM((n * tokens, ff), bf16),
            dma((11,)),
            dma,
            dma,
            dma((2, CHUNKS)),
            dma((2, CHUNKS)),
            dma((2, CHUNKS)),
            dma((2, CHUNKS)),
            dma((CHUNKS,)),
            dma((CHUNKS,)),
            dma((CHUNKS,)),
            dma((CHUNKS,)),
        ],
        compiler_params=pltpu.CompilerParams(
            collective_id=0, has_side_effects=True, vmem_limit_bytes=56 * 1024 * 1024
        ),
        name="layer",
    )(
        queries,
        hidden_in,
        norm_gain,
        route_logits,
        expert_ids,
        new_kv,
        cycle_pos,
        kv_cache,
        out_weight,
        expert_in,
        expert_out,
    )


def on_device(
    hidden_in,
    queries,
    kv_cache,
    new_kv,
    cycle_pos,
    out_weight,
    norm_gain,
    route_logits,
    expert_ids,
    expert_in,
    expert_out,
):
    devices = lax.axis_size("tensor")
    hidden, cache = layer(
        devices,
        queries,
        hidden_in,
        norm_gain.reshape(1, -1),
        route_logits,
        expert_ids,
        new_kv,
        cycle_pos,
        kv_cache,
        (out_weight, expert_in, expert_out),
    )
    return hidden, cache


def solution(mesh):
    return jax.shard_map(
        on_device,
        mesh=mesh,
        in_specs=(
            P(("group", "tensor"), None),
            P(("group", "tensor"), None),
            P(("group", "tensor"), None, None),
            P(("group", "tensor"), None),
            P("group"),
            P("tensor", None),
            P(),
            P(("group", "tensor"), None),
            P(("group", "tensor"), None),
            P("tensor", None, None),
            P("tensor", None, None),
        ),
        out_specs=(P(("group", "tensor"), None), P(("group", "tensor"), None, None)),
        check_vma=False,
    )
```

```python
import functools
import math

import jax
import jax.numpy as jnp
from jax import lax
from jax.experimental import pallas as pl
from jax.experimental.pallas import tpu as pltpu
from jax.sharding import PartitionSpec as P

HD = 128
SINK = 4
MESH = pl.DeviceIdType.MESH


def wait_bytes(ref, sem):
    pltpu.make_async_copy(ref, ref, sem).wait()


CHUNKS = 4


def layer_kernel(
    n,
    queries_hbm,
    hidden_hbm,
    gain_hbm,
    logits_hbm,
    ids_hbm,
    new_kv_hbm,
    cycle_hbm,
    kv_cache,
    out_weight,
    expert_in,
    expert_out,
    hidden_out,
    cache,
    queries,
    hidden_in,
    norm_gain,
    route_logits,
    expert_ids,
    new_kv,
    cycle_pos,
    w_proj,
    w_in,
    w_out,
    query_rows,
    score_rows,
    out_rows,
    by_head,
    heads,
    chip_out,
    chip_in,
    mid,
    gathered,
    gathered_last,
    joined,
    act,
    load_sem,
    swap_send,
    swap_recv,
    head_send,
    head_recv,
    chip_send,
    chip_recv,
    ag_send,
    ag_recv,
):
    me = lax.axis_index("tensor")
    chips = n // 2
    chip, core = me // 2, me % 2
    partner = chip * 2 + (1 - core)
    tokens, width = hidden_in.shape
    ff = w_out.shape[1]
    half = chips * tokens
    part = width // CHUNKS
    f32, bf16 = jnp.float32, jnp.bfloat16

    def peer(step):
        return lax.rem(chip + step, chips)

    barrier = pltpu.get_barrier_semaphore()
    pl.semaphore_signal(barrier, inc=1, device_id={"tensor": partner}, device_id_type=MESH)

    @pl.loop(1, chips)
    def _(step):
        pl.semaphore_signal(
            barrier, inc=1, device_id={"tensor": peer(step) * 2 + core}, device_id_type=MESH
        )

    pairs = (
        (kv_cache, cache),
        (queries_hbm, queries),
        (new_kv_hbm, new_kv),
        (cycle_hbm, cycle_pos),
        (logits_hbm, route_logits),
        (ids_hbm, expert_ids),
        (hidden_hbm, hidden_in),
        (gain_hbm, norm_gain),
        (out_weight, w_proj.at[core]),
        (expert_in.at[0], w_in.at[core]),
        (expert_out.at[0], w_out.at[core]),
    )
    loads = [pltpu.make_async_copy(a, b, load_sem.at[i]) for i, (a, b) in enumerate(pairs)]
    for load in loads[:8]:
        load.start()

    def k_rows(c):
        return pl.ds(c * part, part)

    swapped = [(out_weight, w_proj.at[core])]
    swapped += [
        (expert_in.at[0, k_rows(c)], w_in.at[core, k_rows(c)]) for c in range(CHUNKS)
    ]
    swapped += [(expert_out.at[0], w_out.at[core])]
    swaps = [
        pltpu.make_async_remote_copy(
            src_ref=a,
            dst_ref=b,
            send_sem=swap_send.at[i],
            recv_sem=swap_recv.at[i],
            device_id={"tensor": partner},
            device_id_type=MESH,
        )
        for i, (a, b) in enumerate(swapped)
    ]

    rows_here = cache.shape[0]
    kv_heads = rows_here // tokens
    per_kv = queries.shape[1] // HD
    loads[1].wait()
    for h in range(per_kv):
        query_rows[h * rows_here : (h + 1) * rows_here, :] = queries[
            :, h * HD : (h + 1) * HD
        ].astype(f32)
    for load in (loads[0], loads[2], loads[3]):
        load.wait()
    for load in loads[8:]:
        load.start()
    slot_ids = lax.broadcasted_iota(jnp.int32, cache.shape[1:], 0)
    for t in range(tokens):
        written = slot_ids == cycle_pos[me * tokens + t] + SINK
        for r in range(t * kv_heads, (t + 1) * kv_heads):
            cache[r] = jnp.where(
                written, new_kv[r : r + 1, :].astype(f32), cache[r].astype(f32)
            ).astype(bf16)
    for r in range(rows_here):
        query = query_rows[pl.ds(r, per_kv, stride=rows_here), :].astype(bf16)
        score_rows[r * per_kv : (r + 1) * per_kv, :] = lax.dot_general(
            query,
            cache[r, :, :HD],
            (((1,), (1,)), ((), ())),
            preferred_element_type=f32,
        )
    scores = score_rows[...] / math.sqrt(HD)
    powers = jnp.exp(scores - jnp.max(scores, axis=-1, keepdims=True))
    score_rows[...] = powers / jnp.sum(powers, axis=-1, keepdims=True)
    for r in range(rows_here):
        probs = score_rows[r * per_kv : (r + 1) * per_kv, :].astype(bf16)
        first = (r % kv_heads) * per_kv * tokens + r // kv_heads
        out_rows[pl.ds(first, per_kv, stride=tokens), :] = jnp.dot(
            probs, cache[r, :, HD:], preferred_element_type=f32
        )
    by_head[...] = out_rows[...].reshape(by_head.shape).astype(bf16)

    pl.semaphore_wait(barrier, chips)

    @pl.loop(1, chips)
    def _(step):
        to = peer(step)
        pltpu.make_async_remote_copy(
            src_ref=by_head.at[to],
            dst_ref=heads.at[chip],
            send_sem=head_send,
            recv_sem=head_recv,
            device_id={"tensor": to * 2 + core},
            device_id_type=MESH,
        ).start()

    for swap in swaps:
        swap.start()
    heads[chip] = by_head[chip]

    for load in loads[4:8]:
        load.wait()
    logits = route_logits[...]
    top = logits.shape[1]
    powers = jnp.exp(logits - jnp.max(logits, axis=-1, keepdims=True))
    gate = (powers / jnp.sum(powers, axis=-1, keepdims=True)).astype(bf16).astype(f32)
    pad = gathered_last.shape[2] - part
    lanes = lax.broadcasted_iota(jnp.int32, (tokens, pad), 1)
    ids = expert_ids[...]
    table = jnp.zeros((tokens, pad), f32)
    for j in range(top):
        table = table + jnp.where(lanes == ids[:, j : j + 1], gate[:, j : j + 1], 0.0)

    def block(c):
        return gathered_last if c == CHUNKS - 1 else gathered.at[c]

    def rows_of(ref, lo, hi):
        return ref[:, :, lo:hi].astype(f32).reshape(half, hi - lo)

    def scatter(r, c, rows):
        chip_out[r, c] = rows.reshape(chips, tokens, part).astype(bf16)

        @pl.loop(1, chips)
        def _(step):
            to = peer(step)
            pltpu.make_async_remote_copy(
                src_ref=chip_out.at[r, c, to],
                dst_ref=chip_in.at[r, c, chip],
                send_sem=chip_send.at[r, c],
                recv_sem=chip_recv.at[r, c],
                device_id={"tensor": to * 2 + core},
                device_id_type=MESH,
            ).start()

        chip_in[r, c, chip] = chip_out[r, c, chip]

    def collect(r, c):
        wait_bytes(chip_in.at[r, c, pl.ds(0, chips - 1)], chip_recv.at[r, c])
        return jnp.sum(chip_in[r, c].astype(f32), axis=0)

    wait_bytes(heads.at[pl.ds(0, chips - 1)], head_recv)
    arrived = heads[...].astype(f32)
    head_all = jnp.concatenate(
        [arrived[:, h].reshape(half, HD) for h in range(heads.shape[1])], axis=-1
    ).astype(bf16)
    loads[8].wait()
    swaps[0].wait_recv()
    depth = w_proj.shape[1]
    for c in range(CHUNKS):
        columns = slice(c * part, (c + 1) * part)
        scatter(
            0,
            c,
            jnp.dot(
                head_all,
                w_proj[:, :, columns].reshape(2 * depth, part),
                preferred_element_type=f32,
            ),
        )

    squares = jnp.zeros((tokens, 1), f32)
    for c in range(CHUNKS):
        columns = slice(c * part, (c + 1) * part)
        wide = (hidden_in[:, columns].astype(f32) + collect(0, c)).astype(bf16).astype(f32)
        mid[:, columns] = wide
        squares = squares + jnp.sum(wide * wide, axis=-1, keepdims=True)
        to_send = block(c)
        to_send[chip, :, :part] = (wide * norm_gain[:, columns]).astype(bf16)
        if c == CHUNKS - 1:
            scale = lax.rsqrt(squares / width + 1e-06)
            high = scale.astype(bf16).astype(f32)
            info = jnp.where(lanes == n, high, jnp.where(lanes == n + 1, scale - high, table))
            to_send[chip, :, part:] = info.astype(bf16)

        @pl.loop(1, chips)
        def _(step, c=c, to_send=to_send):
            pltpu.make_async_remote_copy(
                src_ref=to_send.at[chip],
                dst_ref=to_send.at[chip],
                send_sem=ag_send.at[c],
                recv_sem=ag_recv.at[c],
                device_id={"tensor": peer(step) * 2 + core},
                device_id_type=MESH,
            ).start()

    piece = 256

    def product(rows, k, c, lo):
        term = jnp.dot(
            rows,
            w_in[k, c * part : (c + 1) * part, lo : lo + piece],
            preferred_element_type=f32,
        )
        return term if c == 0 else joined[k, :, lo : lo + piece] + term

    last = CHUNKS - 1
    loads[9].wait()
    for c in range(CHUNKS):
        swaps[1 + c].wait_recv()
        wait_bytes(block(c).at[pl.ds(0, chips - 1)], ag_recv.at[c])
        rows = rows_of(block(c), 0, part).astype(bf16)
        if c < last:
            for k in range(2):
                for lo in range(0, 2 * ff, piece):
                    joined[k, :, lo : lo + piece] = product(rows, k, c, lo)
    lane = lax.broadcasted_iota(jnp.int32, (half, pad), 1)
    info = rows_of(block(last), part, part + pad)
    scale = jnp.sum(
        jnp.where((lane == n) | (lane == n + 1), info, 0.0), axis=-1, keepdims=True
    )
    for k in range(2):
        share = jnp.sum(jnp.where(lane == chip * 2 + k, info, 0.0), axis=-1, keepdims=True)
        for lo in range(0, ff, piece):
            gate_part = product(rows, k, last, lo) * scale
            up_part = product(rows, k, last, ff + lo) * scale
            act[:, k * ff + lo : k * ff + lo + piece] = (
                gate_part / (1.0 + jnp.exp(-gate_part)) * up_part * share
            ).astype(bf16)
    loads[10].wait()
    swaps[1 + CHUNKS].wait_recv()
    for c in range(CHUNKS):
        scatter(
            1,
            c,
            jnp.dot(
                act[...],
                w_out[:, :, c * part : (c + 1) * part].reshape(2 * ff, part),
                preferred_element_type=f32,
            ),
        )
    for c in range(CHUNKS):
        columns = slice(c * part, (c + 1) * part)
        hidden_out[:, columns] = (mid[:, columns] + collect(1, c)).astype(bf16)

    wait_bytes(heads.at[pl.ds(0, chips - 1)], head_send)
    for swap in swaps:
        swap.wait_send()
    for c in range(CHUNKS):
        for r in range(2):
            wait_bytes(chip_out.at[r, c, pl.ds(0, chips - 1)], chip_send.at[r, c])
        wait_bytes(block(c).at[pl.ds(0, chips - 1)], ag_send.at[c])


def layer(n, queries, hidden_in, norm_gain, route_logits, expert_ids, new_kv, cycle_pos, kv_cache, weights):
    tokens, width = hidden_in.shape
    out_weight, expert_in, expert_out = weights
    ff = expert_out.shape[1]
    chips = n // 2
    part = width // CHUNKS
    pad = -(-(n + 2) // 128) * 128
    rows_here, slots, _ = kv_cache.shape
    heads_all = rows_here // tokens * (queries.shape[1] // HD)
    exchange = (chips, heads_all // chips, tokens, HD)
    bf16, f32 = jnp.bfloat16, jnp.float32
    hbm = pl.BlockSpec(memory_space=pl.ANY)
    vmem = pl.BlockSpec(memory_space=pltpu.VMEM)
    dma = pltpu.SemaphoreType.DMA
    small = (queries, hidden_in, norm_gain, route_logits, expert_ids, new_kv)
    return pl.pallas_call(
        functools.partial(layer_kernel, n),
        out_shape=(
            pltpu.VMEM((tokens, width), bf16),
            pltpu.VMEM(kv_cache.shape, bf16),
        ),
        in_specs=[hbm] * 11,
        out_specs=(vmem, vmem),
        scratch_shapes=[pltpu.VMEM(a.shape, a.dtype) for a in small]
        + [
            pltpu.SMEM(cycle_pos.shape, cycle_pos.dtype),
            pltpu.VMEM((2,) + out_weight.shape, bf16),
            pltpu.VMEM((2,) + expert_in.shape[1:], bf16),
            pltpu.VMEM((2,) + expert_out.shape[1:], bf16),
            pltpu.VMEM((heads_all * tokens, HD), f32),
            pltpu.VMEM((heads_all * tokens, slots), f32),
            pltpu.VMEM((heads_all * tokens, HD), f32),
            pltpu.VMEM(exchange, bf16),
            pltpu.VMEM(exchange, bf16),
            pltpu.VMEM((2, CHUNKS, chips, tokens, part), bf16),
            pltpu.VMEM((2, CHUNKS, chips, tokens, part), bf16),
            pltpu.VMEM((tokens, width), f32),
            pltpu.VMEM((CHUNKS - 1, chips, tokens, part), bf16),
            pltpu.VMEM((chips, tokens, part + pad), bf16),
            pltpu.VMEM((2, chips * tokens, 2 * ff), f32),
            pltpu.VMEM((chips * tokens, 2 * ff), bf16),
            dma((11,)),
            dma((CHUNKS + 2,)),
            dma((CHUNKS + 2,)),
            dma,
            dma,
            dma((2, CHUNKS)),
            dma((2, CHUNKS)),
            dma((CHUNKS,)),
            dma((CHUNKS,)),
        ],
        compiler_params=pltpu.CompilerParams(
            collective_id=0, has_side_effects=True, vmem_limit_bytes=56 * 1024 * 1024
        ),
        name="layer",
    )(
        queries,
        hidden_in,
        norm_gain,
        route_logits,
        expert_ids,
        new_kv,
        cycle_pos,
        kv_cache,
        out_weight,
        expert_in,
        expert_out,
    )


def on_device(
    hidden_in,
    queries,
    kv_cache,
    new_kv,
    cycle_pos,
    out_weight,
    norm_gain,
    route_logits,
    expert_ids,
    expert_in,
    expert_out,
):
    devices = lax.axis_size("tensor")
    hidden, cache = layer(
        devices,
        queries,
        hidden_in,
        norm_gain.reshape(1, -1),
        route_logits,
        expert_ids,
        new_kv,
        cycle_pos,
        kv_cache,
        (out_weight, expert_in, expert_out),
    )
    return hidden, cache


def solution(mesh):
    return jax.shard_map(
        on_device,
        mesh=mesh,
        in_specs=(
            P(("group", "tensor"), None),
            P(("group", "tensor"), None),
            P(("group", "tensor"), None, None),
            P(("group", "tensor"), None),
            P("group"),
            P("tensor", None),
            P(),
            P(("group", "tensor"), None),
            P(("group", "tensor"), None),
            P("tensor", None, None),
            P("tensor", None, None),
        ),
        out_specs=(P(("group", "tensor"), None), P(("group", "tensor"), None, None)),
        check_vma=False,
    )
```

```python
import functools
import math

import jax
import jax.numpy as jnp
from jax import lax
from jax.experimental import pallas as pl
from jax.experimental.pallas import tpu as pltpu
from jax.sharding import PartitionSpec as P

HD = 128
SINK = 4
MESH = pl.DeviceIdType.MESH


def wait_bytes(ref, sem):
    pltpu.make_async_copy(ref, ref, sem).wait()


CHUNKS = 4
HALVED = ((1,), (1,), (1,))


def layer_kernel(
    n,
    queries_hbm,
    hidden_hbm,
    gain_hbm,
    logits_hbm,
    ids_hbm,
    new_kv_hbm,
    cycle_hbm,
    kv_cache,
    out_weight,
    expert_in,
    expert_out,
    hidden_out,
    cache,
    queries,
    hidden_in,
    norm_gain,
    route_logits,
    expert_ids,
    new_kv,
    cycle_pos,
    w_proj,
    w_in,
    w_out,
    query_rows,
    score_rows,
    out_rows,
    by_head,
    heads,
    chip_out,
    chip_in,
    mid,
    gathered,
    gathered_last,
    joined,
    act,
    load_sem,
    swap_send,
    swap_recv,
    head_send,
    head_recv,
    chip_send,
    chip_recv,
    ag_send,
    ag_recv,
    far_in,
    far_out,
    far_recv,
    cross_recv,
):
    me = lax.axis_index("tensor")
    chips = n // 2
    chip, core = me // 2, me % 2
    partner = chip * 2 + (1 - core)
    tokens, width = hidden_in.shape
    ff = w_out.shape[1]
    half = chips * tokens
    part = width // CHUNKS
    f32, bf16 = jnp.float32, jnp.bfloat16

    halved_gather, *halved_sum = HALVED
    near_count = chips // 2
    base = chip // near_count * near_count
    mirror = lax.rem(chip + near_count, chips)

    def peer(step):
        return lax.rem(chip + step, chips)

    def near(step):
        return base + lax.rem(chip - base + step, near_count)

    def of_cores(cores, first, second):
        for number in range(2):
            pl.when(core == number)(first if number in cores else second)

    def send_to(to, src, dst, send_sem, recv_sem):
        pltpu.make_async_remote_copy(
            src_ref=src,
            dst_ref=dst,
            send_sem=send_sem,
            recv_sem=recv_sem,
            device_id={"tensor": to * 2 + core},
            device_id_type=MESH,
        ).start()

    barrier = pltpu.get_barrier_semaphore()
    pl.semaphore_signal(barrier, inc=1, device_id={"tensor": partner}, device_id_type=MESH)

    @pl.loop(1, chips)
    def _(step):
        pl.semaphore_signal(
            barrier, inc=1, device_id={"tensor": peer(step) * 2 + core}, device_id_type=MESH
        )

    pairs = (
        (kv_cache, cache),
        (queries_hbm, queries),
        (new_kv_hbm, new_kv),
        (cycle_hbm, cycle_pos),
        (logits_hbm, route_logits),
        (ids_hbm, expert_ids),
        (hidden_hbm, hidden_in),
        (gain_hbm, norm_gain),
        (out_weight, w_proj.at[core]),
        (expert_in.at[0], w_in.at[core]),
        (expert_out.at[0], w_out.at[core]),
    )
    loads = [pltpu.make_async_copy(a, b, load_sem.at[i]) for i, (a, b) in enumerate(pairs)]
    for load in loads[:8]:
        load.start()

    def k_rows(c):
        return pl.ds(c * part, part)

    swapped = [(out_weight, w_proj.at[core])]
    swapped += [
        (expert_in.at[0, k_rows(c)], w_in.at[core, k_rows(c)]) for c in range(CHUNKS)
    ]
    swapped += [(expert_out.at[0], w_out.at[core])]
    swaps = [
        pltpu.make_async_remote_copy(
            src_ref=a,
            dst_ref=b,
            send_sem=swap_send.at[i],
            recv_sem=swap_recv.at[i],
            device_id={"tensor": partner},
            device_id_type=MESH,
        )
        for i, (a, b) in enumerate(swapped)
    ]

    rows_here = cache.shape[0]
    kv_heads = rows_here // tokens
    per_kv = queries.shape[1] // HD
    loads[1].wait()
    for h in range(per_kv):
        query_rows[h * rows_here : (h + 1) * rows_here, :] = queries[
            :, h * HD : (h + 1) * HD
        ].astype(f32)
    for load in (loads[0], loads[2], loads[3]):
        load.wait()
    for load in loads[8:]:
        load.start()
    slot_ids = lax.broadcasted_iota(jnp.int32, cache.shape[1:], 0)
    for t in range(tokens):
        written = slot_ids == cycle_pos[me * tokens + t] + SINK
        for r in range(t * kv_heads, (t + 1) * kv_heads):
            cache[r] = jnp.where(
                written, new_kv[r : r + 1, :].astype(f32), cache[r].astype(f32)
            ).astype(bf16)
    for r in range(rows_here):
        query = query_rows[pl.ds(r, per_kv, stride=rows_here), :].astype(bf16)
        score_rows[r * per_kv : (r + 1) * per_kv, :] = lax.dot_general(
            query,
            cache[r, :, :HD],
            (((1,), (1,)), ((), ())),
            preferred_element_type=f32,
        )
    scores = score_rows[...] / math.sqrt(HD)
    powers = jnp.exp(scores - jnp.max(scores, axis=-1, keepdims=True))
    score_rows[...] = powers / jnp.sum(powers, axis=-1, keepdims=True)
    for r in range(rows_here):
        probs = score_rows[r * per_kv : (r + 1) * per_kv, :].astype(bf16)
        first = (r % kv_heads) * per_kv * tokens + r // kv_heads
        out_rows[pl.ds(first, per_kv, stride=tokens), :] = jnp.dot(
            probs, cache[r, :, HD:], preferred_element_type=f32
        )
    by_head[...] = out_rows[...].reshape(by_head.shape).astype(bf16)

    for r in range(2):

        def clear(r=r):
            @pl.loop(1, near_count)
            def _(step):
                slot = lax.rem(near(step) + near_count, chips)
                for c in range(CHUNKS):
                    chip_in[r, c, slot] = jnp.zeros((tokens, part), bf16)

        of_cores(halved_sum[r], clear, lambda: None)
    pl.semaphore_wait(barrier, chips)

    @pl.loop(1, chips)
    def _(step):
        to = peer(step)
        pltpu.make_async_remote_copy(
            src_ref=by_head.at[to],
            dst_ref=heads.at[chip],
            send_sem=head_send,
            recv_sem=head_recv,
            device_id={"tensor": to * 2 + core},
            device_id_type=MESH,
        ).start()

    for swap in swaps:
        swap.start()
    heads[chip] = by_head[chip]

    for load in loads[4:8]:
        load.wait()
    logits = route_logits[...]
    top = logits.shape[1]
    powers = jnp.exp(logits - jnp.max(logits, axis=-1, keepdims=True))
    gate = (powers / jnp.sum(powers, axis=-1, keepdims=True)).astype(bf16).astype(f32)
    pad = gathered_last.shape[2] - part
    lanes = lax.broadcasted_iota(jnp.int32, (tokens, pad), 1)
    ids = expert_ids[...]
    table = jnp.zeros((tokens, pad), f32)
    for j in range(top):
        table = table + jnp.where(lanes == ids[:, j : j + 1], gate[:, j : j + 1], 0.0)

    def block(c):
        return gathered_last if c == CHUNKS - 1 else gathered.at[c]

    def rows_of(ref, lo, hi):
        return ref[:, :, lo:hi].astype(f32).reshape(half, hi - lo)

    def scatter(r, c, rows):
        chip_out[r, c] = rows.reshape(chips, tokens, part).astype(bf16)
        out, sent = chip_out.at[r, c], chip_send.at[r, c]

        def block_to(to):
            send_to(to, out.at[to], chip_in.at[r, c, chip], sent, chip_recv.at[r, c])

        def direct():
            @pl.loop(1, chips)
            def _(step):
                block_to(peer(step))

        def halved():
            @pl.loop(1, near_count)
            def _(step):
                to = near(step)
                beyond = lax.rem(to + near_count, chips)
                send_to(to, out.at[beyond], far_in.at[r, c, chip - base], sent, far_recv.at[r, c])

            @pl.loop(1, near_count)
            def _(step):
                block_to(near(step))

        of_cores(halved_sum[r], halved, direct)
        chip_in[r, c, chip] = chip_out[r, c, chip]

    def cross(r, c):
        def halved():
            far_in[r, c, chip - base] = chip_out[r, c, mirror]
            wait_bytes(far_in.at[r, c, pl.ds(0, near_count - 1)], far_recv.at[r, c])
            far_out[r, c] = jnp.sum(far_in[r, c].astype(f32), axis=0).astype(bf16)
            send_to(
                mirror,
                far_out.at[r, c],
                chip_in.at[r, c, chip],
                chip_send.at[r, c],
                chip_recv.at[r, c],
            )

        of_cores(halved_sum[r], halved, lambda: None)

    def collect(r, c):
        of_cores(
            halved_sum[r],
            lambda: wait_bytes(chip_in.at[r, c, pl.ds(0, near_count)], chip_recv.at[r, c]),
            lambda: wait_bytes(chip_in.at[r, c, pl.ds(0, chips - 1)], chip_recv.at[r, c]),
        )
        return jnp.sum(chip_in[r, c].astype(f32), axis=0)

    wait_bytes(heads.at[pl.ds(0, chips - 1)], head_recv)
    arrived = heads[...].astype(f32)
    head_all = jnp.concatenate(
        [arrived[:, h].reshape(half, HD) for h in range(heads.shape[1])], axis=-1
    ).astype(bf16)
    loads[8].wait()
    swaps[0].wait_recv()
    depth = w_proj.shape[1]
    for c in range(CHUNKS):
        columns = slice(c * part, (c + 1) * part)
        scatter(
            0,
            c,
            jnp.dot(
                head_all,
                w_proj[:, :, columns].reshape(2 * depth, part),
                preferred_element_type=f32,
            ),
        )

    for c in range(CHUNKS):
        cross(0, c)
    squares = jnp.zeros((tokens, 1), f32)
    for c in range(CHUNKS):
        columns = slice(c * part, (c + 1) * part)
        wide = (hidden_in[:, columns].astype(f32) + collect(0, c)).astype(bf16).astype(f32)
        mid[:, columns] = wide
        squares = squares + jnp.sum(wide * wide, axis=-1, keepdims=True)
        to_send = block(c)
        to_send[chip, :, :part] = (wide * norm_gain[:, columns]).astype(bf16)
        if c == CHUNKS - 1:
            scale = lax.rsqrt(squares / width + 1e-06)
            high = scale.astype(bf16).astype(f32)
            info = jnp.where(lanes == n, high, jnp.where(lanes == n + 1, scale - high, table))
            to_send[chip, :, part:] = info.astype(bf16)

        def direct(c=c, mine=to_send.at[chip]):
            @pl.loop(1, chips)
            def _(step):
                send_to(peer(step), mine, mine, ag_send.at[c], ag_recv.at[c])

        def halved(c=c, mine=to_send.at[chip]):
            send_to(mirror, mine, mine, ag_send.at[c], cross_recv.at[c])

            @pl.loop(1, near_count)
            def _(step):
                send_to(near(step), mine, mine, ag_send.at[c], ag_recv.at[c])

        of_cores(halved_gather, halved, direct)

    def forward(c):
        def halved():
            theirs = block(c).at[mirror]
            wait_bytes(theirs, cross_recv.at[c])

            @pl.loop(1, near_count)
            def _(step):
                send_to(near(step), theirs, theirs, ag_send.at[c], ag_recv.at[c])

        of_cores(halved_gather, halved, lambda: None)

    for c in range(CHUNKS):
        forward(c)

    piece = 256

    def product(rows, k, c, lo):
        term = jnp.dot(
            rows,
            w_in[k, c * part : (c + 1) * part, lo : lo + piece],
            preferred_element_type=f32,
        )
        return term if c == 0 else joined[k, :, lo : lo + piece] + term

    last = CHUNKS - 1
    loads[9].wait()
    for c in range(CHUNKS):
        swaps[1 + c].wait_recv()
        of_cores(
            halved_gather,
            lambda c=c: wait_bytes(block(c).at[pl.ds(0, chips - 2)], ag_recv.at[c]),
            lambda c=c: wait_bytes(block(c).at[pl.ds(0, chips - 1)], ag_recv.at[c]),
        )
        rows = rows_of(block(c), 0, part).astype(bf16)
        if c < last:
            for k in range(2):
                for lo in range(0, 2 * ff, piece):
                    joined[k, :, lo : lo + piece] = product(rows, k, c, lo)
    lane = lax.broadcasted_iota(jnp.int32, (half, pad), 1)
    info = rows_of(block(last), part, part + pad)
    scale = jnp.sum(
        jnp.where((lane == n) | (lane == n + 1), info, 0.0), axis=-1, keepdims=True
    )
    for k in range(2):
        share = jnp.sum(jnp.where(lane == chip * 2 + k, info, 0.0), axis=-1, keepdims=True)
        for lo in range(0, ff, piece):
            gate_part = product(rows, k, last, lo) * scale
            up_part = product(rows, k, last, ff + lo) * scale
            act[:, k * ff + lo : k * ff + lo + piece] = (
                gate_part / (1.0 + jnp.exp(-gate_part)) * up_part * share
            ).astype(bf16)
    loads[10].wait()
    swaps[1 + CHUNKS].wait_recv()
    for c in range(CHUNKS):
        scatter(
            1,
            c,
            jnp.dot(
                act[...],
                w_out[:, :, c * part : (c + 1) * part].reshape(2 * ff, part),
                preferred_element_type=f32,
            ),
        )
    for c in range(CHUNKS):
        cross(1, c)
    for c in range(CHUNKS):
        columns = slice(c * part, (c + 1) * part)
        hidden_out[:, columns] = (mid[:, columns] + collect(1, c)).astype(bf16)

    wait_bytes(heads.at[pl.ds(0, chips - 1)], head_send)
    for swap in swaps:
        swap.wait_send()
    for c in range(CHUNKS):
        for r in range(2):
            wait_bytes(chip_out.at[r, c, pl.ds(0, chips - 1)], chip_send.at[r, c])
        wait_bytes(block(c).at[pl.ds(0, chips - 1)], ag_send.at[c])


def layer(n, queries, hidden_in, norm_gain, route_logits, expert_ids, new_kv, cycle_pos, kv_cache, weights):
    tokens, width = hidden_in.shape
    out_weight, expert_in, expert_out = weights
    ff = expert_out.shape[1]
    chips = n // 2
    part = width // CHUNKS
    pad = -(-(n + 2) // 128) * 128
    rows_here, slots, _ = kv_cache.shape
    heads_all = rows_here // tokens * (queries.shape[1] // HD)
    exchange = (chips, heads_all // chips, tokens, HD)
    bf16, f32 = jnp.bfloat16, jnp.float32
    hbm = pl.BlockSpec(memory_space=pl.ANY)
    vmem = pl.BlockSpec(memory_space=pltpu.VMEM)
    dma = pltpu.SemaphoreType.DMA
    small = (queries, hidden_in, norm_gain, route_logits, expert_ids, new_kv)
    return pl.pallas_call(
        functools.partial(layer_kernel, n),
        out_shape=(
            pltpu.VMEM((tokens, width), bf16),
            pltpu.VMEM(kv_cache.shape, bf16),
        ),
        in_specs=[hbm] * 11,
        out_specs=(vmem, vmem),
        scratch_shapes=[pltpu.VMEM(a.shape, a.dtype) for a in small]
        + [
            pltpu.SMEM(cycle_pos.shape, cycle_pos.dtype),
            pltpu.VMEM((2,) + out_weight.shape, bf16),
            pltpu.VMEM((2,) + expert_in.shape[1:], bf16),
            pltpu.VMEM((2,) + expert_out.shape[1:], bf16),
            pltpu.VMEM((heads_all * tokens, HD), f32),
            pltpu.VMEM((heads_all * tokens, slots), f32),
            pltpu.VMEM((heads_all * tokens, HD), f32),
            pltpu.VMEM(exchange, bf16),
            pltpu.VMEM(exchange, bf16),
            pltpu.VMEM((2, CHUNKS, chips, tokens, part), bf16),
            pltpu.VMEM((2, CHUNKS, chips, tokens, part), bf16),
            pltpu.VMEM((tokens, width), f32),
            pltpu.VMEM((CHUNKS - 1, chips, tokens, part), bf16),
            pltpu.VMEM((chips, tokens, part + pad), bf16),
            pltpu.VMEM((2, chips * tokens, 2 * ff), f32),
            pltpu.VMEM((chips * tokens, 2 * ff), bf16),
            dma((11,)),
            dma((CHUNKS + 2,)),
            dma((CHUNKS + 2,)),
            dma,
            dma,
            dma((2, CHUNKS)),
            dma((2, CHUNKS)),
            dma((CHUNKS,)),
            dma((CHUNKS,)),
            pltpu.VMEM((2, CHUNKS, chips // 2, tokens, part), bf16),
            pltpu.VMEM((2, CHUNKS, tokens, part), bf16),
            dma((2, CHUNKS)),
            dma((CHUNKS,)),
        ],
        compiler_params=pltpu.CompilerParams(
            collective_id=0, has_side_effects=True, vmem_limit_bytes=56 * 1024 * 1024
        ),
        name="layer",
    )(
        queries,
        hidden_in,
        norm_gain,
        route_logits,
        expert_ids,
        new_kv,
        cycle_pos,
        kv_cache,
        out_weight,
        expert_in,
        expert_out,
    )


def on_device(
    hidden_in,
    queries,
    kv_cache,
    new_kv,
    cycle_pos,
    out_weight,
    norm_gain,
    route_logits,
    expert_ids,
    expert_in,
    expert_out,
):
    devices = lax.axis_size("tensor")
    hidden, cache = layer(
        devices,
        queries,
        hidden_in,
        norm_gain.reshape(1, -1),
        route_logits,
        expert_ids,
        new_kv,
        cycle_pos,
        kv_cache,
        (out_weight, expert_in, expert_out),
    )
    return hidden, cache


def solution(mesh):
    return jax.shard_map(
        on_device,
        mesh=mesh,
        in_specs=(
            P(("group", "tensor"), None),
            P(("group", "tensor"), None),
            P(("group", "tensor"), None, None),
            P(("group", "tensor"), None),
            P("group"),
            P("tensor", None),
            P(),
            P(("group", "tensor"), None),
            P(("group", "tensor"), None),
            P("tensor", None, None),
            P("tensor", None, None),
        ),
        out_specs=(P(("group", "tensor"), None), P(("group", "tensor"), None, None)),
        check_vma=False,
    )
```

```python
import functools
import math

import jax
import jax.numpy as jnp
from jax import lax
from jax.experimental import pallas as pl
from jax.experimental.pallas import tpu as pltpu
from jax.sharding import PartitionSpec as P

HD = 128
SINK = 4
MESH = pl.DeviceIdType.MESH


def wait_bytes(ref, sem):
    pltpu.make_async_copy(ref, ref, sem).wait()


CHUNKS = (4, 1)
HALVED = ((1,), (1,), (1,))


def layer_kernel(
    n,
    queries_hbm,
    hidden_hbm,
    gain_hbm,
    logits_hbm,
    ids_hbm,
    new_kv_hbm,
    cycle_hbm,
    kv_cache,
    out_weight,
    expert_in,
    expert_out,
    hidden_out,
    cache,
    queries,
    hidden_in,
    norm_gain,
    route_logits,
    expert_ids,
    new_kv,
    cycle_pos,
    w_proj,
    w_in,
    w_out,
    query_rows,
    score_rows,
    out_rows,
    by_head,
    heads,
    chip_out_a,
    chip_out_b,
    chip_in_a,
    chip_in_b,
    mid,
    gathered,
    gathered_last,
    joined,
    act,
    load_sem,
    swap_send,
    swap_recv,
    head_send,
    head_recv,
    chip_send_a,
    chip_send_b,
    chip_recv_a,
    chip_recv_b,
    ag_send,
    ag_recv,
    far_in_a,
    far_in_b,
    far_out_a,
    far_out_b,
    far_recv_a,
    far_recv_b,
    cross_recv,
):
    me = lax.axis_index("tensor")
    chips = n // 2
    chip, core = me // 2, me % 2
    partner = chip * 2 + (1 - core)
    tokens, width = hidden_in.shape
    ff = w_out.shape[1]
    half = chips * tokens
    parts = [width // count for count in CHUNKS]
    part = parts[0]
    chip_out, chip_in = (chip_out_a, chip_out_b), (chip_in_a, chip_in_b)
    far_in, far_out, far_recv = (far_in_a, far_in_b), (far_out_a, far_out_b), (far_recv_a, far_recv_b)
    chip_send, chip_recv = (chip_send_a, chip_send_b), (chip_recv_a, chip_recv_b)
    f32, bf16 = jnp.float32, jnp.bfloat16

    halved_gather, *halved_sum = HALVED
    near_count = chips // 2
    base = chip // near_count * near_count
    mirror = lax.rem(chip + near_count, chips)

    def peer(step):
        return lax.rem(chip + step, chips)

    def near(step):
        return base + lax.rem(chip - base + step, near_count)

    def of_cores(cores, first, second):
        for number in range(2):
            pl.when(core == number)(first if number in cores else second)

    def send_to(to, src, dst, send_sem, recv_sem):
        pltpu.make_async_remote_copy(
            src_ref=src,
            dst_ref=dst,
            send_sem=send_sem,
            recv_sem=recv_sem,
            device_id={"tensor": to * 2 + core},
            device_id_type=MESH,
        ).start()

    barrier = pltpu.get_barrier_semaphore()
    pl.semaphore_signal(barrier, inc=1, device_id={"tensor": partner}, device_id_type=MESH)

    @pl.loop(1, chips)
    def _(step):
        pl.semaphore_signal(
            barrier, inc=1, device_id={"tensor": peer(step) * 2 + core}, device_id_type=MESH
        )

    pairs = (
        (kv_cache, cache),
        (queries_hbm, queries),
        (new_kv_hbm, new_kv),
        (cycle_hbm, cycle_pos),
        (logits_hbm, route_logits),
        (ids_hbm, expert_ids),
        (hidden_hbm, hidden_in),
        (gain_hbm, norm_gain),
        (out_weight, w_proj.at[core]),
        (expert_in.at[0], w_in.at[core]),
        (expert_out.at[0], w_out.at[core]),
    )
    loads = [pltpu.make_async_copy(a, b, load_sem.at[i]) for i, (a, b) in enumerate(pairs)]
    for load in loads[:8]:
        load.start()

    def k_rows(c):
        return pl.ds(c * part, part)

    swapped = [(out_weight, w_proj.at[core])]
    swapped += [
        (expert_in.at[0, k_rows(c)], w_in.at[core, k_rows(c)]) for c in range(CHUNKS[0])
    ]
    swapped += [(expert_out.at[0], w_out.at[core])]
    swaps = [
        pltpu.make_async_remote_copy(
            src_ref=a,
            dst_ref=b,
            send_sem=swap_send.at[i],
            recv_sem=swap_recv.at[i],
            device_id={"tensor": partner},
            device_id_type=MESH,
        )
        for i, (a, b) in enumerate(swapped)
    ]

    rows_here = cache.shape[0]
    kv_heads = rows_here // tokens
    per_kv = queries.shape[1] // HD
    loads[1].wait()
    for h in range(per_kv):
        query_rows[h * rows_here : (h + 1) * rows_here, :] = queries[
            :, h * HD : (h + 1) * HD
        ].astype(f32)
    for load in (loads[0], loads[2], loads[3]):
        load.wait()
    for load in loads[8:]:
        load.start()
    slot_ids = lax.broadcasted_iota(jnp.int32, cache.shape[1:], 0)
    for t in range(tokens):
        written = slot_ids == cycle_pos[me * tokens + t] + SINK
        for r in range(t * kv_heads, (t + 1) * kv_heads):
            cache[r] = jnp.where(
                written, new_kv[r : r + 1, :].astype(f32), cache[r].astype(f32)
            ).astype(bf16)
    for r in range(rows_here):
        query = query_rows[pl.ds(r, per_kv, stride=rows_here), :].astype(bf16)
        score_rows[r * per_kv : (r + 1) * per_kv, :] = lax.dot_general(
            query,
            cache[r, :, :HD],
            (((1,), (1,)), ((), ())),
            preferred_element_type=f32,
        )
    scores = score_rows[...] / math.sqrt(HD)
    powers = jnp.exp(scores - jnp.max(scores, axis=-1, keepdims=True))
    score_rows[...] = powers / jnp.sum(powers, axis=-1, keepdims=True)
    for r in range(rows_here):
        probs = score_rows[r * per_kv : (r + 1) * per_kv, :].astype(bf16)
        first = (r % kv_heads) * per_kv * tokens + r // kv_heads
        out_rows[pl.ds(first, per_kv, stride=tokens), :] = jnp.dot(
            probs, cache[r, :, HD:], preferred_element_type=f32
        )
    by_head[...] = out_rows[...].reshape(by_head.shape).astype(bf16)

    for r in range(2):

        def clear(r=r):
            @pl.loop(1, near_count)
            def _(step):
                slot = lax.rem(near(step) + near_count, chips)
                for c in range(CHUNKS[r]):
                    chip_in[r][c, slot] = jnp.zeros((tokens, parts[r]), bf16)

        of_cores(halved_sum[r], clear, lambda: None)
    pl.semaphore_wait(barrier, chips)

    @pl.loop(1, chips)
    def _(step):
        to = peer(step)
        pltpu.make_async_remote_copy(
            src_ref=by_head.at[to],
            dst_ref=heads.at[chip],
            send_sem=head_send,
            recv_sem=head_recv,
            device_id={"tensor": to * 2 + core},
            device_id_type=MESH,
        ).start()

    for swap in swaps:
        swap.start()
    heads[chip] = by_head[chip]

    for load in loads[4:8]:
        load.wait()
    logits = route_logits[...]
    top = logits.shape[1]
    powers = jnp.exp(logits - jnp.max(logits, axis=-1, keepdims=True))
    gate = (powers / jnp.sum(powers, axis=-1, keepdims=True)).astype(bf16).astype(f32)
    pad = gathered_last.shape[2] - part
    lanes = lax.broadcasted_iota(jnp.int32, (tokens, pad), 1)
    ids = expert_ids[...]
    table = jnp.zeros((tokens, pad), f32)
    for j in range(top):
        table = table + jnp.where(lanes == ids[:, j : j + 1], gate[:, j : j + 1], 0.0)

    def block(c):
        return gathered_last if c == CHUNKS[0] - 1 else gathered.at[c]

    def rows_of(ref, lo, hi):
        return ref[:, :, lo:hi].astype(f32).reshape(half, hi - lo)

    def scatter(r, c, rows):
        chip_out[r][c] = rows.reshape(chips, tokens, parts[r]).astype(bf16)
        out, sent = chip_out[r].at[c], chip_send[r].at[c]

        def block_to(to):
            send_to(to, out.at[to], chip_in[r].at[c, chip], sent, chip_recv[r].at[c])

        def direct():
            @pl.loop(1, chips)
            def _(step):
                block_to(peer(step))

        def halved():
            @pl.loop(1, near_count)
            def _(step):
                to = near(step)
                beyond = lax.rem(to + near_count, chips)
                send_to(to, out.at[beyond], far_in[r].at[c, chip - base], sent, far_recv[r].at[c])

            @pl.loop(1, near_count)
            def _(step):
                block_to(near(step))

        of_cores(halved_sum[r], halved, direct)
        chip_in[r][c, chip] = chip_out[r][c, chip]

    def cross(r, c):
        def halved():
            far_in[r][c, chip - base] = chip_out[r][c, mirror]
            wait_bytes(far_in[r].at[c, pl.ds(0, near_count - 1)], far_recv[r].at[c])
            far_out[r][c] = jnp.sum(far_in[r][c].astype(f32), axis=0).astype(bf16)
            send_to(
                mirror,
                far_out[r].at[c],
                chip_in[r].at[c, chip],
                chip_send[r].at[c],
                chip_recv[r].at[c],
            )

        of_cores(halved_sum[r], halved, lambda: None)

    def collect(r, c):
        of_cores(
            halved_sum[r],
            lambda: wait_bytes(chip_in[r].at[c, pl.ds(0, near_count)], chip_recv[r].at[c]),
            lambda: wait_bytes(chip_in[r].at[c, pl.ds(0, chips - 1)], chip_recv[r].at[c]),
        )
        return jnp.sum(chip_in[r][c].astype(f32), axis=0)

    wait_bytes(heads.at[pl.ds(0, chips - 1)], head_recv)
    arrived = heads[...].astype(f32)
    head_all = jnp.concatenate(
        [arrived[:, h].reshape(half, HD) for h in range(heads.shape[1])], axis=-1
    ).astype(bf16)
    loads[8].wait()
    swaps[0].wait_recv()
    depth = w_proj.shape[1]
    for c in range(CHUNKS[0]):
        columns = slice(c * part, (c + 1) * part)
        scatter(
            0,
            c,
            jnp.dot(
                head_all,
                w_proj[:, :, columns].reshape(2 * depth, part),
                preferred_element_type=f32,
            ),
        )

    for c in range(CHUNKS[0]):
        cross(0, c)
    squares = jnp.zeros((tokens, 1), f32)
    for c in range(CHUNKS[0]):
        columns = slice(c * part, (c + 1) * part)
        wide = (hidden_in[:, columns].astype(f32) + collect(0, c)).astype(bf16).astype(f32)
        mid[:, columns] = wide
        squares = squares + jnp.sum(wide * wide, axis=-1, keepdims=True)
        to_send = block(c)
        to_send[chip, :, :part] = (wide * norm_gain[:, columns]).astype(bf16)
        if c == CHUNKS[0] - 1:
            scale = lax.rsqrt(squares / width + 1e-06)
            high = scale.astype(bf16).astype(f32)
            info = jnp.where(lanes == n, high, jnp.where(lanes == n + 1, scale - high, table))
            to_send[chip, :, part:] = info.astype(bf16)

        def direct(c=c, mine=to_send.at[chip]):
            @pl.loop(1, chips)
            def _(step):
                send_to(peer(step), mine, mine, ag_send.at[c], ag_recv.at[c])

        def halved(c=c, mine=to_send.at[chip]):
            send_to(mirror, mine, mine, ag_send.at[c], cross_recv.at[c])

            @pl.loop(1, near_count)
            def _(step):
                send_to(near(step), mine, mine, ag_send.at[c], ag_recv.at[c])

        of_cores(halved_gather, halved, direct)

    def forward(c):
        def halved():
            theirs = block(c).at[mirror]
            wait_bytes(theirs, cross_recv.at[c])

            @pl.loop(1, near_count)
            def _(step):
                send_to(near(step), theirs, theirs, ag_send.at[c], ag_recv.at[c])

        of_cores(halved_gather, halved, lambda: None)

    for c in range(CHUNKS[0]):
        forward(c)

    piece = 256

    def product(rows, k, c, lo):
        term = jnp.dot(
            rows,
            w_in[k, c * part : (c + 1) * part, lo : lo + piece],
            preferred_element_type=f32,
        )
        return term if c == 0 else joined[k, :, lo : lo + piece] + term

    last = CHUNKS[0] - 1
    loads[9].wait()
    for c in range(CHUNKS[0]):
        swaps[1 + c].wait_recv()
        of_cores(
            halved_gather,
            lambda c=c: wait_bytes(block(c).at[pl.ds(0, chips - 2)], ag_recv.at[c]),
            lambda c=c: wait_bytes(block(c).at[pl.ds(0, chips - 1)], ag_recv.at[c]),
        )
        rows = rows_of(block(c), 0, part).astype(bf16)
        if c < last:
            for k in range(2):
                for lo in range(0, 2 * ff, piece):
                    joined[k, :, lo : lo + piece] = product(rows, k, c, lo)
    lane = lax.broadcasted_iota(jnp.int32, (half, pad), 1)
    info = rows_of(block(last), part, part + pad)
    scale = jnp.sum(
        jnp.where((lane == n) | (lane == n + 1), info, 0.0), axis=-1, keepdims=True
    )
    for k in range(2):
        share = jnp.sum(jnp.where(lane == chip * 2 + k, info, 0.0), axis=-1, keepdims=True)
        for lo in range(0, ff, piece):
            gate_part = product(rows, k, last, lo) * scale
            up_part = product(rows, k, last, ff + lo) * scale
            act[:, k * ff + lo : k * ff + lo + piece] = (
                gate_part / (1.0 + jnp.exp(-gate_part)) * up_part * share
            ).astype(bf16)
    loads[10].wait()
    swaps[-1].wait_recv()
    for c in range(CHUNKS[1]):
        scatter(
            1,
            c,
            jnp.dot(
                act[...],
                w_out[:, :, c * parts[1] : (c + 1) * parts[1]].reshape(2 * ff, parts[1]),
                preferred_element_type=f32,
            ),
        )
    for c in range(CHUNKS[1]):
        cross(1, c)
    for c in range(CHUNKS[1]):
        columns = slice(c * parts[1], (c + 1) * parts[1])
        hidden_out[:, columns] = (mid[:, columns] + collect(1, c)).astype(bf16)

    wait_bytes(heads.at[pl.ds(0, chips - 1)], head_send)
    for swap in swaps:
        swap.wait_send()
    for r in range(2):
        for c in range(CHUNKS[r]):
            wait_bytes(chip_out[r].at[c, pl.ds(0, chips - 1)], chip_send[r].at[c])
    for c in range(CHUNKS[0]):
        wait_bytes(block(c).at[pl.ds(0, chips - 1)], ag_send.at[c])


def layer(n, queries, hidden_in, norm_gain, route_logits, expert_ids, new_kv, cycle_pos, kv_cache, weights):
    tokens, width = hidden_in.shape
    out_weight, expert_in, expert_out = weights
    ff = expert_out.shape[1]
    chips = n // 2
    parts = [width // count for count in CHUNKS]
    part = parts[0]
    both = tuple(zip(CHUNKS, parts))
    pad = -(-(n + 2) // 128) * 128
    rows_here, slots, _ = kv_cache.shape
    heads_all = rows_here // tokens * (queries.shape[1] // HD)
    exchange = (chips, heads_all // chips, tokens, HD)
    bf16, f32 = jnp.bfloat16, jnp.float32
    hbm = pl.BlockSpec(memory_space=pl.ANY)
    vmem = pl.BlockSpec(memory_space=pltpu.VMEM)
    dma = pltpu.SemaphoreType.DMA
    small = (queries, hidden_in, norm_gain, route_logits, expert_ids, new_kv)
    return pl.pallas_call(
        functools.partial(layer_kernel, n),
        out_shape=(
            pltpu.VMEM((tokens, width), bf16),
            pltpu.VMEM(kv_cache.shape, bf16),
        ),
        in_specs=[hbm] * 11,
        out_specs=(vmem, vmem),
        scratch_shapes=[pltpu.VMEM(a.shape, a.dtype) for a in small]
        + [
            pltpu.SMEM(cycle_pos.shape, cycle_pos.dtype),
            pltpu.VMEM((2,) + out_weight.shape, bf16),
            pltpu.VMEM((2,) + expert_in.shape[1:], bf16),
            pltpu.VMEM((2,) + expert_out.shape[1:], bf16),
            pltpu.VMEM((heads_all * tokens, HD), f32),
            pltpu.VMEM((heads_all * tokens, slots), f32),
            pltpu.VMEM((heads_all * tokens, HD), f32),
            pltpu.VMEM(exchange, bf16),
            pltpu.VMEM(exchange, bf16),
            *[pltpu.VMEM((c, chips, tokens, p), bf16) for c, p in both],
            *[pltpu.VMEM((c, chips, tokens, p), bf16) for c, p in both],
            pltpu.VMEM((tokens, width), f32),
            pltpu.VMEM((CHUNKS[0] - 1, chips, tokens, part), bf16),
            pltpu.VMEM((chips, tokens, part + pad), bf16),
            pltpu.VMEM((2, chips * tokens, 2 * ff), f32),
            pltpu.VMEM((chips * tokens, 2 * ff), bf16),
            dma((11,)),
            dma((CHUNKS[0] + 2,)),
            dma((CHUNKS[0] + 2,)),
            dma,
            dma,
            *[dma((c,)) for c in CHUNKS],
            *[dma((c,)) for c in CHUNKS],
            dma((CHUNKS[0],)),
            dma((CHUNKS[0],)),
            *[pltpu.VMEM((c, chips // 2, tokens, p), bf16) for c, p in both],
            *[pltpu.VMEM((c, tokens, p), bf16) for c, p in both],
            *[dma((c,)) for c in CHUNKS],
            dma((CHUNKS[0],)),
        ],
        compiler_params=pltpu.CompilerParams(
            collective_id=0, has_side_effects=True, vmem_limit_bytes=56 * 1024 * 1024
        ),
        name="layer",
    )(
        queries,
        hidden_in,
        norm_gain,
        route_logits,
        expert_ids,
        new_kv,
        cycle_pos,
        kv_cache,
        out_weight,
        expert_in,
        expert_out,
    )


def on_device(
    hidden_in,
    queries,
    kv_cache,
    new_kv,
    cycle_pos,
    out_weight,
    norm_gain,
    route_logits,
    expert_ids,
    expert_in,
    expert_out,
):
    devices = lax.axis_size("tensor")
    hidden, cache = layer(
        devices,
        queries,
        hidden_in,
        norm_gain.reshape(1, -1),
        route_logits,
        expert_ids,
        new_kv,
        cycle_pos,
        kv_cache,
        (out_weight, expert_in, expert_out),
    )
    return hidden, cache


def solution(mesh):
    return jax.shard_map(
        on_device,
        mesh=mesh,
        in_specs=(
            P(("group", "tensor"), None),
            P(("group", "tensor"), None),
            P(("group", "tensor"), None, None),
            P(("group", "tensor"), None),
            P("group"),
            P("tensor", None),
            P(),
            P(("group", "tensor"), None),
            P(("group", "tensor"), None),
            P("tensor", None, None),
            P("tensor", None, None),
        ),
        out_specs=(P(("group", "tensor"), None), P(("group", "tensor"), None, None)),
        check_vma=False,
    )
```

```python
import functools
import math

import jax
import jax.numpy as jnp
from jax import lax
from jax.experimental import pallas as pl
from jax.experimental.pallas import tpu as pltpu
from jax.sharding import PartitionSpec as P

HD = 128
SINK = 4
MESH = pl.DeviceIdType.MESH


def wait_bytes(ref, sem):
    pltpu.make_async_copy(ref, ref, sem).wait()


CHUNKS = (4, 1)
HALVED = ((1,), (1,), (1,))


def layer_kernel(
    n,
    queries_hbm,
    hidden_hbm,
    gain_hbm,
    logits_hbm,
    ids_hbm,
    new_kv_hbm,
    cycle_hbm,
    kv_cache,
    out_weight,
    expert_in,
    expert_out,
    hidden_out,
    cache,
    queries,
    hidden_in,
    norm_gain,
    route_logits,
    expert_ids,
    new_kv,
    cycle_pos,
    w_proj,
    w_in,
    w_out,
    query_rows,
    score_rows,
    out_rows,
    by_head,
    heads,
    chip_out_a,
    chip_out_b,
    chip_in_a,
    chip_in_b,
    mid,
    gathered,
    gathered_last,
    joined,
    act,
    load_sem,
    swap_send,
    swap_recv,
    head_send,
    head_recv,
    chip_send_a,
    chip_send_b,
    chip_recv_a,
    chip_recv_b,
    ag_send,
    ag_recv,
    far_in_a,
    far_in_b,
    far_out_a,
    far_out_b,
    far_recv_a,
    far_recv_b,
    cross_recv,
):
    me = lax.axis_index("tensor")
    chips = n // 2
    chip, core = me // 2, me % 2
    partner = chip * 2 + (1 - core)
    tokens, width = hidden_in.shape
    ff = w_out.shape[1]
    half = chips * tokens
    parts = [width // count for count in CHUNKS]
    part = parts[0]
    chip_out, chip_in = (chip_out_a, chip_out_b), (chip_in_a, chip_in_b)
    far_in, far_out, far_recv = (far_in_a, far_in_b), (far_out_a, far_out_b), (far_recv_a, far_recv_b)
    chip_send, chip_recv = (chip_send_a, chip_send_b), (chip_recv_a, chip_recv_b)
    f32, bf16 = jnp.float32, jnp.bfloat16

    halved_gather, *halved_sum = HALVED
    near_count = chips // 2
    base = chip // near_count * near_count
    mirror = lax.rem(chip + near_count, chips)

    def peer(step):
        return lax.rem(chip + step, chips)

    def facing(step):
        return lax.bitwise_xor(chip, chips - step) if chips & (chips - 1) == 0 else peer(step)

    def near(step):
        return base + lax.rem(chip - base + step, near_count)

    def of_cores(cores, first, second):
        for number in range(2):
            pl.when(core == number)(first if number in cores else second)

    def send_to(to, src, dst, send_sem, recv_sem):
        pltpu.make_async_remote_copy(
            src_ref=src,
            dst_ref=dst,
            send_sem=send_sem,
            recv_sem=recv_sem,
            device_id={"tensor": to * 2 + core},
            device_id_type=MESH,
        ).start()

    barrier = pltpu.get_barrier_semaphore()
    pl.semaphore_signal(barrier, inc=1, device_id={"tensor": partner}, device_id_type=MESH)

    @pl.loop(1, chips)
    def _(step):
        pl.semaphore_signal(
            barrier, inc=1, device_id={"tensor": peer(step) * 2 + core}, device_id_type=MESH
        )

    pairs = (
        (kv_cache, cache),
        (queries_hbm, queries),
        (new_kv_hbm, new_kv),
        (cycle_hbm, cycle_pos),
        (logits_hbm, route_logits),
        (ids_hbm, expert_ids),
        (hidden_hbm, hidden_in),
        (gain_hbm, norm_gain),
        (out_weight, w_proj.at[core]),
        (expert_in.at[0], w_in.at[core]),
        (expert_out.at[0], w_out.at[core]),
    )
    loads = [pltpu.make_async_copy(a, b, load_sem.at[i]) for i, (a, b) in enumerate(pairs)]
    for load in loads[:8]:
        load.start()

    def k_rows(c):
        return pl.ds(c * part, part)

    swapped = [(out_weight, w_proj.at[core])]
    swapped += [
        (expert_in.at[0, k_rows(c)], w_in.at[core, k_rows(c)]) for c in range(CHUNKS[0])
    ]
    swapped += [(expert_out.at[0], w_out.at[core])]
    swaps = [
        pltpu.make_async_remote_copy(
            src_ref=a,
            dst_ref=b,
            send_sem=swap_send.at[i],
            recv_sem=swap_recv.at[i],
            device_id={"tensor": partner},
            device_id_type=MESH,
        )
        for i, (a, b) in enumerate(swapped)
    ]

    rows_here = cache.shape[0]
    kv_heads = rows_here // tokens
    per_kv = queries.shape[1] // HD
    loads[1].wait()
    for h in range(per_kv):
        query_rows[h * rows_here : (h + 1) * rows_here, :] = queries[
            :, h * HD : (h + 1) * HD
        ].astype(f32)
    for load in (loads[0], loads[2], loads[3]):
        load.wait()
    for load in loads[8:]:
        load.start()
    slot_ids = lax.broadcasted_iota(jnp.int32, cache.shape[1:], 0)
    for t in range(tokens):
        written = slot_ids == cycle_pos[me * tokens + t] + SINK
        for r in range(t * kv_heads, (t + 1) * kv_heads):
            cache[r] = jnp.where(
                written, new_kv[r : r + 1, :].astype(f32), cache[r].astype(f32)
            ).astype(bf16)
    for r in range(rows_here):
        query = query_rows[pl.ds(r, per_kv, stride=rows_here), :].astype(bf16)
        score_rows[r * per_kv : (r + 1) * per_kv, :] = lax.dot_general(
            query,
            cache[r, :, :HD],
            (((1,), (1,)), ((), ())),
            preferred_element_type=f32,
        )
    scores = score_rows[...] / math.sqrt(HD)
    powers = jnp.exp(scores - jnp.max(scores, axis=-1, keepdims=True))
    score_rows[...] = powers / jnp.sum(powers, axis=-1, keepdims=True)
    for r in range(rows_here):
        probs = score_rows[r * per_kv : (r + 1) * per_kv, :].astype(bf16)
        first = (r % kv_heads) * per_kv * tokens + r // kv_heads
        out_rows[pl.ds(first, per_kv, stride=tokens), :] = jnp.dot(
            probs, cache[r, :, HD:], preferred_element_type=f32
        )
    by_head[...] = out_rows[...].reshape(by_head.shape).astype(bf16)

    for r in range(2):

        def clear(r=r):
            @pl.loop(1, near_count)
            def _(step):
                slot = lax.rem(near(step) + near_count, chips)
                for c in range(CHUNKS[r]):
                    chip_in[r][c, slot] = jnp.zeros((tokens, parts[r]), bf16)

        of_cores(halved_sum[r], clear, lambda: None)
    pl.semaphore_wait(barrier, chips)

    @pl.loop(1, chips)
    def _(step):
        to = facing(step)
        pltpu.make_async_remote_copy(
            src_ref=by_head.at[to],
            dst_ref=heads.at[chip],
            send_sem=head_send,
            recv_sem=head_recv,
            device_id={"tensor": to * 2 + core},
            device_id_type=MESH,
        ).start()

    for swap in swaps:
        swap.start()
    heads[chip] = by_head[chip]

    for load in loads[4:8]:
        load.wait()
    logits = route_logits[...]
    top = logits.shape[1]
    powers = jnp.exp(logits - jnp.max(logits, axis=-1, keepdims=True))
    gate = (powers / jnp.sum(powers, axis=-1, keepdims=True)).astype(bf16).astype(f32)
    pad = gathered_last.shape[2] - part
    lanes = lax.broadcasted_iota(jnp.int32, (tokens, pad), 1)
    ids = expert_ids[...]
    table = jnp.zeros((tokens, pad), f32)
    for j in range(top):
        table = table + jnp.where(lanes == ids[:, j : j + 1], gate[:, j : j + 1], 0.0)

    def block(c):
        return gathered_last if c == CHUNKS[0] - 1 else gathered.at[c]

    def rows_of(ref, lo, hi):
        return ref[:, :, lo:hi].astype(f32).reshape(half, hi - lo)

    def scatter(r, c, rows):
        chip_out[r][c] = rows.reshape(chips, tokens, parts[r]).astype(bf16)
        out, sent = chip_out[r].at[c], chip_send[r].at[c]

        def block_to(to):
            send_to(to, out.at[to], chip_in[r].at[c, chip], sent, chip_recv[r].at[c])

        def direct():
            @pl.loop(1, chips)
            def _(step):
                block_to(facing(step) if r == 0 else peer(step))

        def halved():
            @pl.loop(1, near_count)
            def _(step):
                to = near(step)
                beyond = lax.rem(to + near_count, chips)
                send_to(to, out.at[beyond], far_in[r].at[c, chip - base], sent, far_recv[r].at[c])

            @pl.loop(1, near_count)
            def _(step):
                block_to(near(step))

        of_cores(halved_sum[r], halved, direct)
        chip_in[r][c, chip] = chip_out[r][c, chip]

    def cross(r, c):
        def halved():
            far_in[r][c, chip - base] = chip_out[r][c, mirror]
            wait_bytes(far_in[r].at[c, pl.ds(0, near_count - 1)], far_recv[r].at[c])
            far_out[r][c] = jnp.sum(far_in[r][c].astype(f32), axis=0).astype(bf16)
            send_to(
                mirror,
                far_out[r].at[c],
                chip_in[r].at[c, chip],
                chip_send[r].at[c],
                chip_recv[r].at[c],
            )

        of_cores(halved_sum[r], halved, lambda: None)

    def collect(r, c):
        of_cores(
            halved_sum[r],
            lambda: wait_bytes(chip_in[r].at[c, pl.ds(0, near_count)], chip_recv[r].at[c]),
            lambda: wait_bytes(chip_in[r].at[c, pl.ds(0, chips - 1)], chip_recv[r].at[c]),
        )
        return jnp.sum(chip_in[r][c].astype(f32), axis=0)

    wait_bytes(heads.at[pl.ds(0, chips - 1)], head_recv)
    arrived = heads[...].astype(f32)
    head_all = jnp.concatenate(
        [arrived[:, h].reshape(half, HD) for h in range(heads.shape[1])], axis=-1
    ).astype(bf16)
    loads[8].wait()
    swaps[0].wait_recv()
    depth = w_proj.shape[1]
    for c in range(CHUNKS[0]):
        columns = slice(c * part, (c + 1) * part)
        scatter(
            0,
            c,
            jnp.dot(
                head_all,
                w_proj[:, :, columns].reshape(2 * depth, part),
                preferred_element_type=f32,
            ),
        )

    for c in range(CHUNKS[0]):
        cross(0, c)
    squares = jnp.zeros((tokens, 1), f32)
    for c in range(CHUNKS[0]):
        columns = slice(c * part, (c + 1) * part)
        wide = (hidden_in[:, columns].astype(f32) + collect(0, c)).astype(bf16).astype(f32)
        mid[:, columns] = wide
        squares = squares + jnp.sum(wide * wide, axis=-1, keepdims=True)
        to_send = block(c)
        to_send[chip, :, :part] = (wide * norm_gain[:, columns]).astype(bf16)
        if c == CHUNKS[0] - 1:
            scale = lax.rsqrt(squares / width + 1e-06)
            high = scale.astype(bf16).astype(f32)
            info = jnp.where(lanes == n, high, jnp.where(lanes == n + 1, scale - high, table))
            to_send[chip, :, part:] = info.astype(bf16)

        def direct(c=c, mine=to_send.at[chip]):
            @pl.loop(1, chips)
            def _(step):
                send_to(facing(step), mine, mine, ag_send.at[c], ag_recv.at[c])

        def halved(c=c, mine=to_send.at[chip]):
            send_to(mirror, mine, mine, ag_send.at[c], cross_recv.at[c])

            @pl.loop(1, near_count)
            def _(step):
                send_to(near(step), mine, mine, ag_send.at[c], ag_recv.at[c])

        of_cores(halved_gather, halved, direct)

    def forward(c):
        def halved():
            theirs = block(c).at[mirror]
            wait_bytes(theirs, cross_recv.at[c])

            @pl.loop(1, near_count)
            def _(step):
                send_to(near(step), theirs, theirs, ag_send.at[c], ag_recv.at[c])

        of_cores(halved_gather, halved, lambda: None)

    for c in range(CHUNKS[0]):
        forward(c)

    piece = 256

    def product(rows, k, c, lo):
        term = jnp.dot(
            rows,
            w_in[k, c * part : (c + 1) * part, lo : lo + piece],
            preferred_element_type=f32,
        )
        return term if c == 0 else joined[k, :, lo : lo + piece] + term

    last = CHUNKS[0] - 1
    loads[9].wait()
    for c in range(CHUNKS[0]):
        swaps[1 + c].wait_recv()
        of_cores(
            halved_gather,
            lambda c=c: wait_bytes(block(c).at[pl.ds(0, chips - 2)], ag_recv.at[c]),
            lambda c=c: wait_bytes(block(c).at[pl.ds(0, chips - 1)], ag_recv.at[c]),
        )
        rows = rows_of(block(c), 0, part).astype(bf16)
        if c < last:
            for k in range(2):
                for lo in range(0, 2 * ff, piece):
                    joined[k, :, lo : lo + piece] = product(rows, k, c, lo)
    lane = lax.broadcasted_iota(jnp.int32, (half, pad), 1)
    info = rows_of(block(last), part, part + pad)
    scale = jnp.sum(
        jnp.where((lane == n) | (lane == n + 1), info, 0.0), axis=-1, keepdims=True
    )
    for k in range(2):
        share = jnp.sum(jnp.where(lane == chip * 2 + k, info, 0.0), axis=-1, keepdims=True)
        for lo in range(0, ff, piece):
            gate_part = product(rows, k, last, lo) * scale
            up_part = product(rows, k, last, ff + lo) * scale
            act[:, k * ff + lo : k * ff + lo + piece] = (
                gate_part / (1.0 + jnp.exp(-gate_part)) * up_part * share
            ).astype(bf16)
    loads[10].wait()
    swaps[-1].wait_recv()
    for c in range(CHUNKS[1]):
        scatter(
            1,
            c,
            jnp.dot(
                act[...],
                w_out[:, :, c * parts[1] : (c + 1) * parts[1]].reshape(2 * ff, parts[1]),
                preferred_element_type=f32,
            ),
        )
    for c in range(CHUNKS[1]):
        cross(1, c)
    for c in range(CHUNKS[1]):
        columns = slice(c * parts[1], (c + 1) * parts[1])
        hidden_out[:, columns] = (mid[:, columns] + collect(1, c)).astype(bf16)

    wait_bytes(heads.at[pl.ds(0, chips - 1)], head_send)
    for swap in swaps:
        swap.wait_send()
    for r in range(2):
        for c in range(CHUNKS[r]):
            wait_bytes(chip_out[r].at[c, pl.ds(0, chips - 1)], chip_send[r].at[c])
    for c in range(CHUNKS[0]):
        wait_bytes(block(c).at[pl.ds(0, chips - 1)], ag_send.at[c])


def layer(n, queries, hidden_in, norm_gain, route_logits, expert_ids, new_kv, cycle_pos, kv_cache, weights):
    tokens, width = hidden_in.shape
    out_weight, expert_in, expert_out = weights
    ff = expert_out.shape[1]
    chips = n // 2
    parts = [width // count for count in CHUNKS]
    part = parts[0]
    both = tuple(zip(CHUNKS, parts))
    pad = -(-(n + 2) // 128) * 128
    rows_here, slots, _ = kv_cache.shape
    heads_all = rows_here // tokens * (queries.shape[1] // HD)
    exchange = (chips, heads_all // chips, tokens, HD)
    bf16, f32 = jnp.bfloat16, jnp.float32
    hbm = pl.BlockSpec(memory_space=pl.ANY)
    vmem = pl.BlockSpec(memory_space=pltpu.VMEM)
    dma = pltpu.SemaphoreType.DMA
    small = (queries, hidden_in, norm_gain, route_logits, expert_ids, new_kv)
    return pl.pallas_call(
        functools.partial(layer_kernel, n),
        out_shape=(
            pltpu.VMEM((tokens, width), bf16),
            pltpu.VMEM(kv_cache.shape, bf16),
        ),
        in_specs=[hbm] * 11,
        out_specs=(vmem, vmem),
        scratch_shapes=[pltpu.VMEM(a.shape, a.dtype) for a in small]
        + [
            pltpu.SMEM(cycle_pos.shape, cycle_pos.dtype),
            pltpu.VMEM((2,) + out_weight.shape, bf16),
            pltpu.VMEM((2,) + expert_in.shape[1:], bf16),
            pltpu.VMEM((2,) + expert_out.shape[1:], bf16),
            pltpu.VMEM((heads_all * tokens, HD), f32),
            pltpu.VMEM((heads_all * tokens, slots), f32),
            pltpu.VMEM((heads_all * tokens, HD), f32),
            pltpu.VMEM(exchange, bf16),
            pltpu.VMEM(exchange, bf16),
            *[pltpu.VMEM((c, chips, tokens, p), bf16) for c, p in both],
            *[pltpu.VMEM((c, chips, tokens, p), bf16) for c, p in both],
            pltpu.VMEM((tokens, width), f32),
            pltpu.VMEM((CHUNKS[0] - 1, chips, tokens, part), bf16),
            pltpu.VMEM((chips, tokens, part + pad), bf16),
            pltpu.VMEM((2, chips * tokens, 2 * ff), f32),
            pltpu.VMEM((chips * tokens, 2 * ff), bf16),
            dma((11,)),
            dma((CHUNKS[0] + 2,)),
            dma((CHUNKS[0] + 2,)),
            dma,
            dma,
            *[dma((c,)) for c in CHUNKS],
            *[dma((c,)) for c in CHUNKS],
            dma((CHUNKS[0],)),
            dma((CHUNKS[0],)),
            *[pltpu.VMEM((c, chips // 2, tokens, p), bf16) for c, p in both],
            *[pltpu.VMEM((c, tokens, p), bf16) for c, p in both],
            *[dma((c,)) for c in CHUNKS],
            dma((CHUNKS[0],)),
        ],
        compiler_params=pltpu.CompilerParams(
            collective_id=0, has_side_effects=True, vmem_limit_bytes=56 * 1024 * 1024
        ),
        name="layer",
    )(
        queries,
        hidden_in,
        norm_gain,
        route_logits,
        expert_ids,
        new_kv,
        cycle_pos,
        kv_cache,
        out_weight,
        expert_in,
        expert_out,
    )


def store_kernel(hidden, cache, hidden_out, new_cache, sems):
    copies = (
        pltpu.make_async_copy(cache, new_cache, sems.at[1]),
        pltpu.make_async_copy(hidden, hidden_out, sems.at[0]),
    )
    for copy in copies:
        copy.start()
    for copy in copies:
        copy.wait()


def store(hidden, cache):
    anywhere = pl.BlockSpec(memory_space=pl.ANY)
    return pl.pallas_call(
        store_kernel,
        out_shape=tuple(jax.ShapeDtypeStruct(a.shape, a.dtype) for a in (hidden, cache)),
        in_specs=[pl.BlockSpec(memory_space=pltpu.VMEM)] * 2,
        out_specs=(anywhere,) * 2,
        scratch_shapes=[pltpu.SemaphoreType.DMA((2,))],
        name="store",
    )(*(pltpu.with_memory_space_constraint(a, pltpu.VMEM) for a in (hidden, cache)))


def on_device(
    hidden_in,
    queries,
    kv_cache,
    new_kv,
    cycle_pos,
    out_weight,
    norm_gain,
    route_logits,
    expert_ids,
    expert_in,
    expert_out,
):
    devices = lax.axis_size("tensor")
    hidden, cache = layer(
        devices,
        queries,
        hidden_in,
        norm_gain.reshape(1, -1),
        route_logits,
        expert_ids,
        new_kv,
        cycle_pos,
        kv_cache,
        (out_weight, expert_in, expert_out),
    )
    return store(hidden, cache)


def solution(mesh):
    return jax.shard_map(
        on_device,
        mesh=mesh,
        in_specs=(
            P(("group", "tensor"), None),
            P(("group", "tensor"), None),
            P(("group", "tensor"), None, None),
            P(("group", "tensor"), None),
            P("group"),
            P("tensor", None),
            P(),
            P(("group", "tensor"), None),
            P(("group", "tensor"), None),
            P("tensor", None, None),
            P("tensor", None, None),
        ),
        out_specs=(P(("group", "tensor"), None), P(("group", "tensor"), None, None)),
        check_vma=False,
    )
```

```python
import functools
import math

import jax
import jax.numpy as jnp
from jax import lax
from jax.experimental import pallas as pl
from jax.experimental.pallas import tpu as pltpu
from jax.sharding import PartitionSpec as P

HD = 128
SINK = 4
MESH = pl.DeviceIdType.MESH


def wait_bytes(ref, sem):
    pltpu.make_async_copy(ref, ref, sem).wait()


CHUNKS = (4, 1)
PIECES = (1, 2)
HALVED = ((1,), (1,), (1,))


def layer_kernel(
    n,
    queries_hbm,
    hidden_hbm,
    gain_hbm,
    logits_hbm,
    ids_hbm,
    new_kv_hbm,
    cycle_hbm,
    kv_cache,
    out_weight,
    expert_in,
    expert_out,
    hidden_out,
    cache,
    queries,
    hidden_in,
    norm_gain,
    route_logits,
    expert_ids,
    new_kv,
    cycle_pos,
    w_proj,
    w_in,
    w_out,
    query_rows,
    score_rows,
    out_rows,
    by_head,
    heads,
    chip_out_a,
    chip_out_b,
    chip_in_a,
    chip_in_b,
    mid,
    gathered,
    gathered_last,
    joined,
    act,
    load_sem,
    swap_send,
    swap_recv,
    head_send,
    head_recv,
    chip_send_a,
    chip_send_b,
    chip_recv_a,
    chip_recv_b,
    ag_send,
    ag_recv,
    far_in_a,
    far_in_b,
    far_out_a,
    far_out_b,
    far_recv_a,
    far_recv_b,
    cross_recv,
):
    me = lax.axis_index("tensor")
    chips = n // 2
    chip, core = me // 2, me % 2
    partner = chip * 2 + (1 - core)
    tokens, width = hidden_in.shape
    ff = w_out.shape[1]
    half = chips * tokens
    parts = [width // count for count in CHUNKS]
    part = parts[0]
    chip_out, chip_in = (chip_out_a, chip_out_b), (chip_in_a, chip_in_b)
    far_in, far_out, far_recv = (far_in_a, far_in_b), (far_out_a, far_out_b), (far_recv_a, far_recv_b)
    chip_send, chip_recv = (chip_send_a, chip_send_b), (chip_recv_a, chip_recv_b)
    f32, bf16 = jnp.float32, jnp.bfloat16

    halved_gather, *halved_sum = HALVED
    near_count = chips // 2
    base = chip // near_count * near_count
    mirror = lax.rem(chip + near_count, chips)

    def peer(step):
        return lax.rem(chip + step, chips)

    def facing(step):
        return lax.bitwise_xor(chip, chips - step) if chips & (chips - 1) == 0 else peer(step)

    def near(step):
        return base + lax.rem(chip - base + step, near_count)

    def of_cores(cores, first, second):
        for number in range(2):
            pl.when(core == number)(first if number in cores else second)

    def send_to(to, src, dst, send_sem, recv_sem):
        pltpu.make_async_remote_copy(
            src_ref=src,
            dst_ref=dst,
            send_sem=send_sem,
            recv_sem=recv_sem,
            device_id={"tensor": to * 2 + core},
            device_id_type=MESH,
        ).start()

    barrier = pltpu.get_barrier_semaphore()
    pl.semaphore_signal(barrier, inc=1, device_id={"tensor": partner}, device_id_type=MESH)

    @pl.loop(1, chips)
    def _(step):
        pl.semaphore_signal(
            barrier, inc=1, device_id={"tensor": peer(step) * 2 + core}, device_id_type=MESH
        )

    pairs = (
        (kv_cache, cache),
        (queries_hbm, queries),
        (new_kv_hbm, new_kv),
        (cycle_hbm, cycle_pos),
        (logits_hbm, route_logits),
        (ids_hbm, expert_ids),
        (hidden_hbm, hidden_in),
        (gain_hbm, norm_gain),
        (out_weight, w_proj.at[core]),
        (expert_in.at[0], w_in.at[core]),
        (expert_out.at[0], w_out.at[core]),
    )
    loads = [pltpu.make_async_copy(a, b, load_sem.at[i]) for i, (a, b) in enumerate(pairs)]
    for load in loads[:8]:
        load.start()

    def k_rows(c):
        return pl.ds(c * part, part)

    swapped = [(out_weight, w_proj.at[core])]
    swapped += [
        (expert_in.at[0, k_rows(c)], w_in.at[core, k_rows(c)]) for c in range(CHUNKS[0])
    ]
    for p in range(PIECES[1]):
        columns = pl.ds(p * (width // PIECES[1]), width // PIECES[1])
        swapped += [(expert_out.at[0, :, columns], w_out.at[core, :, columns])]
    swaps = [
        pltpu.make_async_remote_copy(
            src_ref=a,
            dst_ref=b,
            send_sem=swap_send.at[i],
            recv_sem=swap_recv.at[i],
            device_id={"tensor": partner},
            device_id_type=MESH,
        )
        for i, (a, b) in enumerate(swapped)
    ]

    rows_here = cache.shape[0]
    kv_heads = rows_here // tokens
    per_kv = queries.shape[1] // HD
    loads[1].wait()
    for h in range(per_kv):
        query_rows[h * rows_here : (h + 1) * rows_here, :] = queries[
            :, h * HD : (h + 1) * HD
        ].astype(f32)
    for load in (loads[0], loads[2], loads[3]):
        load.wait()
    for load in loads[8:]:
        load.start()
    slot_ids = lax.broadcasted_iota(jnp.int32, cache.shape[1:], 0)
    for t in range(tokens):
        written = slot_ids == cycle_pos[me * tokens + t] + SINK
        for r in range(t * kv_heads, (t + 1) * kv_heads):
            cache[r] = jnp.where(
                written, new_kv[r : r + 1, :].astype(f32), cache[r].astype(f32)
            ).astype(bf16)
    for r in range(rows_here):
        query = query_rows[pl.ds(r, per_kv, stride=rows_here), :].astype(bf16)
        score_rows[r * per_kv : (r + 1) * per_kv, :] = lax.dot_general(
            query,
            cache[r, :, :HD],
            (((1,), (1,)), ((), ())),
            preferred_element_type=f32,
        )
    scores = score_rows[...] / math.sqrt(HD)
    powers = jnp.exp(scores - jnp.max(scores, axis=-1, keepdims=True))
    score_rows[...] = powers / jnp.sum(powers, axis=-1, keepdims=True)
    for r in range(rows_here):
        probs = score_rows[r * per_kv : (r + 1) * per_kv, :].astype(bf16)
        first = (r % kv_heads) * per_kv * tokens + r // kv_heads
        out_rows[pl.ds(first, per_kv, stride=tokens), :] = jnp.dot(
            probs, cache[r, :, HD:], preferred_element_type=f32
        )
    by_head[...] = out_rows[...].reshape(by_head.shape).astype(bf16)

    for r in range(2):

        def clear(r=r):
            @pl.loop(1, near_count)
            def _(step):
                slot = lax.rem(near(step) + near_count, chips)
                for c in range(CHUNKS[r]):
                    chip_in[r][c, slot] = jnp.zeros((tokens, parts[r]), bf16)

        of_cores(halved_sum[r], clear, lambda: None)
    pl.semaphore_wait(barrier, chips)

    @pl.loop(1, chips)
    def _(step):
        to = facing(step)
        pltpu.make_async_remote_copy(
            src_ref=by_head.at[to],
            dst_ref=heads.at[chip],
            send_sem=head_send,
            recv_sem=head_recv,
            device_id={"tensor": to * 2 + core},
            device_id_type=MESH,
        ).start()

    for swap in swaps:
        swap.start()
    heads[chip] = by_head[chip]

    for load in loads[4:8]:
        load.wait()
    logits = route_logits[...]
    top = logits.shape[1]
    powers = jnp.exp(logits - jnp.max(logits, axis=-1, keepdims=True))
    gate = (powers / jnp.sum(powers, axis=-1, keepdims=True)).astype(bf16).astype(f32)
    pad = gathered_last.shape[2] - part
    lanes = lax.broadcasted_iota(jnp.int32, (tokens, pad), 1)
    ids = expert_ids[...]
    table = jnp.zeros((tokens, pad), f32)
    for j in range(top):
        table = table + jnp.where(lanes == ids[:, j : j + 1], gate[:, j : j + 1], 0.0)

    def block(c):
        return gathered_last if c == CHUNKS[0] - 1 else gathered.at[c]

    def rows_of(ref, lo, hi):
        return ref[:, :, lo:hi].astype(f32).reshape(half, hi - lo)

    def cut(r, p):
        step = parts[r] // PIECES[r]
        return pl.ds(p * step, step)

    def put(r, c, p, rows):
        columns = cut(r, p)
        chip_out[r][c, :, :, columns] = rows.reshape(chips, tokens, columns.size).astype(bf16)

        def halved():
            @pl.loop(1, near_count)
            def _(step):
                to = near(step)
                send_to(
                    to,
                    chip_out[r].at[c, lax.rem(to + near_count, chips), :, columns],
                    far_in[r].at[c, chip - base, :, columns],
                    chip_send[r].at[c],
                    far_recv[r].at[c, p],
                )

        of_cores(halved_sum[r], halved, lambda: None)

    def scatter(r, c):
        out, sent = chip_out[r].at[c], chip_send[r].at[c]

        def block_to(to):
            send_to(to, out.at[to], chip_in[r].at[c, chip], sent, chip_recv[r].at[c])

        def direct():
            @pl.loop(1, chips)
            def _(step):
                block_to(facing(step) if r == 0 else peer(step))

        def halved():
            @pl.loop(1, near_count)
            def _(step):
                block_to(near(step))

        of_cores(halved_sum[r], halved, direct)
        chip_in[r][c, chip] = chip_out[r][c, chip]

    def cross(r, c):
        def halved():
            far_in[r][c, chip - base] = chip_out[r][c, mirror]
            for p in range(PIECES[r]):
                columns = cut(r, p)
                wait_bytes(
                    far_in[r].at[c, pl.ds(0, near_count - 1), :, columns], far_recv[r].at[c, p]
                )
                far_out[r][c, :, columns] = jnp.sum(
                    far_in[r][c, :, :, columns].astype(f32), axis=0
                ).astype(bf16)
                send_to(
                    mirror,
                    far_out[r].at[c, :, columns],
                    chip_in[r].at[c, chip, :, columns],
                    chip_send[r].at[c],
                    chip_recv[r].at[c],
                )

        of_cores(halved_sum[r], halved, lambda: None)

    def collect(r, c):
        of_cores(
            halved_sum[r],
            lambda: wait_bytes(chip_in[r].at[c, pl.ds(0, near_count)], chip_recv[r].at[c]),
            lambda: wait_bytes(chip_in[r].at[c, pl.ds(0, chips - 1)], chip_recv[r].at[c]),
        )
        return jnp.sum(chip_in[r][c].astype(f32), axis=0)

    wait_bytes(heads.at[pl.ds(0, chips - 1)], head_recv)
    arrived = heads[...].astype(f32)
    head_all = jnp.concatenate(
        [arrived[:, h].reshape(half, HD) for h in range(heads.shape[1])], axis=-1
    ).astype(bf16)
    loads[8].wait()
    swaps[0].wait_recv()
    depth = w_proj.shape[1]
    for c in range(CHUNKS[0]):
        columns = slice(c * part, (c + 1) * part)
        rows = jnp.dot(
            head_all,
            w_proj[:, :, columns].reshape(2 * depth, part),
            preferred_element_type=f32,
        )
        put(0, c, 0, rows)
        scatter(0, c)

    for c in range(CHUNKS[0]):
        cross(0, c)
    squares = jnp.zeros((tokens, 1), f32)
    for c in range(CHUNKS[0]):
        columns = slice(c * part, (c + 1) * part)
        wide = (hidden_in[:, columns].astype(f32) + collect(0, c)).astype(bf16).astype(f32)
        mid[:, columns] = wide
        squares = squares + jnp.sum(wide * wide, axis=-1, keepdims=True)
        to_send = block(c)
        to_send[chip, :, :part] = (wide * norm_gain[:, columns]).astype(bf16)
        if c == CHUNKS[0] - 1:
            scale = lax.rsqrt(squares / width + 1e-06)
            high = scale.astype(bf16).astype(f32)
            info = jnp.where(lanes == n, high, jnp.where(lanes == n + 1, scale - high, table))
            to_send[chip, :, part:] = info.astype(bf16)

        def direct(c=c, mine=to_send.at[chip]):
            @pl.loop(1, chips)
            def _(step):
                send_to(facing(step), mine, mine, ag_send.at[c], ag_recv.at[c])

        def halved(c=c, mine=to_send.at[chip]):
            send_to(mirror, mine, mine, ag_send.at[c], cross_recv.at[c])

            @pl.loop(1, near_count)
            def _(step):
                send_to(near(step), mine, mine, ag_send.at[c], ag_recv.at[c])

        of_cores(halved_gather, halved, direct)

    def forward(c):
        def halved():
            theirs = block(c).at[mirror]
            wait_bytes(theirs, cross_recv.at[c])

            @pl.loop(1, near_count)
            def _(step):
                send_to(near(step), theirs, theirs, ag_send.at[c], ag_recv.at[c])

        of_cores(halved_gather, halved, lambda: None)

    for c in range(CHUNKS[0]):
        forward(c)

    piece = 256

    def product(rows, k, c, lo):
        term = jnp.dot(
            rows,
            w_in[k, c * part : (c + 1) * part, lo : lo + piece],
            preferred_element_type=f32,
        )
        return term if c == 0 else joined[k, :, lo : lo + piece] + term

    last = CHUNKS[0] - 1
    loads[9].wait()
    for c in range(CHUNKS[0]):
        swaps[1 + c].wait_recv()
        of_cores(
            halved_gather,
            lambda c=c: wait_bytes(block(c).at[pl.ds(0, chips - 2)], ag_recv.at[c]),
            lambda c=c: wait_bytes(block(c).at[pl.ds(0, chips - 1)], ag_recv.at[c]),
        )
        rows = rows_of(block(c), 0, part).astype(bf16)
        if c < last:
            for k in range(2):
                for lo in range(0, 2 * ff, piece):
                    joined[k, :, lo : lo + piece] = product(rows, k, c, lo)
    lane = lax.broadcasted_iota(jnp.int32, (half, pad), 1)
    info = rows_of(block(last), part, part + pad)
    scale = jnp.sum(
        jnp.where((lane == n) | (lane == n + 1), info, 0.0), axis=-1, keepdims=True
    )
    for k in range(2):
        share = jnp.sum(jnp.where(lane == chip * 2 + k, info, 0.0), axis=-1, keepdims=True)
        for lo in range(0, ff, piece):
            gate_part = product(rows, k, last, lo) * scale
            up_part = product(rows, k, last, ff + lo) * scale
            act[:, k * ff + lo : k * ff + lo + piece] = (
                gate_part / (1.0 + jnp.exp(-gate_part)) * up_part * share
            ).astype(bf16)
    loads[10].wait()
    for c in range(CHUNKS[1]):
        for p in range(PIECES[1]):
            swaps[1 + CHUNKS[0] + p].wait_recv()
            columns = cut(1, p)
            low = c * parts[1] + columns.start
            rows = jnp.dot(
                act[...],
                w_out[:, :, low : low + columns.size].reshape(2 * ff, columns.size),
                preferred_element_type=f32,
            )
            put(1, c, p, rows)
        scatter(1, c)
    for c in range(CHUNKS[1]):
        cross(1, c)
    for c in range(CHUNKS[1]):
        columns = slice(c * parts[1], (c + 1) * parts[1])
        hidden_out[:, columns] = (mid[:, columns] + collect(1, c)).astype(bf16)

    wait_bytes(heads.at[pl.ds(0, chips - 1)], head_send)
    for swap in swaps:
        swap.wait_send()
    for r in range(2):
        for c in range(CHUNKS[r]):
            wait_bytes(chip_out[r].at[c, pl.ds(0, chips - 1)], chip_send[r].at[c])
    for c in range(CHUNKS[0]):
        wait_bytes(block(c).at[pl.ds(0, chips - 1)], ag_send.at[c])


def layer(n, queries, hidden_in, norm_gain, route_logits, expert_ids, new_kv, cycle_pos, kv_cache, weights):
    tokens, width = hidden_in.shape
    out_weight, expert_in, expert_out = weights
    ff = expert_out.shape[1]
    chips = n // 2
    parts = [width // count for count in CHUNKS]
    part = parts[0]
    both = tuple(zip(CHUNKS, parts))
    pad = -(-(n + 2) // 128) * 128
    rows_here, slots, _ = kv_cache.shape
    heads_all = rows_here // tokens * (queries.shape[1] // HD)
    exchange = (chips, heads_all // chips, tokens, HD)
    bf16, f32 = jnp.bfloat16, jnp.float32
    hbm = pl.BlockSpec(memory_space=pl.ANY)
    vmem = pl.BlockSpec(memory_space=pltpu.VMEM)
    dma = pltpu.SemaphoreType.DMA
    small = (queries, hidden_in, norm_gain, route_logits, expert_ids, new_kv)
    return pl.pallas_call(
        functools.partial(layer_kernel, n),
        out_shape=(
            pltpu.VMEM((tokens, width), bf16),
            pltpu.VMEM(kv_cache.shape, bf16),
        ),
        in_specs=[hbm] * 11,
        out_specs=(vmem, vmem),
        scratch_shapes=[pltpu.VMEM(a.shape, a.dtype) for a in small]
        + [
            pltpu.SMEM(cycle_pos.shape, cycle_pos.dtype),
            pltpu.VMEM((2,) + out_weight.shape, bf16),
            pltpu.VMEM((2,) + expert_in.shape[1:], bf16),
            pltpu.VMEM((2,) + expert_out.shape[1:], bf16),
            pltpu.VMEM((heads_all * tokens, HD), f32),
            pltpu.VMEM((heads_all * tokens, slots), f32),
            pltpu.VMEM((heads_all * tokens, HD), f32),
            pltpu.VMEM(exchange, bf16),
            pltpu.VMEM(exchange, bf16),
            *[pltpu.VMEM((c, chips, tokens, p), bf16) for c, p in both],
            *[pltpu.VMEM((c, chips, tokens, p), bf16) for c, p in both],
            pltpu.VMEM((tokens, width), f32),
            pltpu.VMEM((CHUNKS[0] - 1, chips, tokens, part), bf16),
            pltpu.VMEM((chips, tokens, part + pad), bf16),
            pltpu.VMEM((2, chips * tokens, 2 * ff), f32),
            pltpu.VMEM((chips * tokens, 2 * ff), bf16),
            dma((11,)),
            dma((CHUNKS[0] + 1 + PIECES[1],)),
            dma((CHUNKS[0] + 1 + PIECES[1],)),
            dma,
            dma,
            *[dma((c,)) for c in CHUNKS],
            *[dma((c,)) for c in CHUNKS],
            dma((CHUNKS[0],)),
            dma((CHUNKS[0],)),
            *[pltpu.VMEM((c, chips // 2, tokens, p), bf16) for c, p in both],
            *[pltpu.VMEM((c, tokens, p), bf16) for c, p in both],
            *[dma((c, p)) for c, p in zip(CHUNKS, PIECES)],
            dma((CHUNKS[0],)),
        ],
        compiler_params=pltpu.CompilerParams(
            collective_id=0, has_side_effects=True, vmem_limit_bytes=56 * 1024 * 1024
        ),
        name="layer",
    )(
        queries,
        hidden_in,
        norm_gain,
        route_logits,
        expert_ids,
        new_kv,
        cycle_pos,
        kv_cache,
        out_weight,
        expert_in,
        expert_out,
    )


def store_kernel(hidden, cache, hidden_out, new_cache, sems):
    copies = (
        pltpu.make_async_copy(cache, new_cache, sems.at[1]),
        pltpu.make_async_copy(hidden, hidden_out, sems.at[0]),
    )
    for copy in copies:
        copy.start()
    for copy in copies:
        copy.wait()


def store(hidden, cache):
    anywhere = pl.BlockSpec(memory_space=pl.ANY)
    return pl.pallas_call(
        store_kernel,
        out_shape=tuple(jax.ShapeDtypeStruct(a.shape, a.dtype) for a in (hidden, cache)),
        in_specs=[pl.BlockSpec(memory_space=pltpu.VMEM)] * 2,
        out_specs=(anywhere,) * 2,
        scratch_shapes=[pltpu.SemaphoreType.DMA((2,))],
        name="store",
    )(*(pltpu.with_memory_space_constraint(a, pltpu.VMEM) for a in (hidden, cache)))


def on_device(
    hidden_in,
    queries,
    kv_cache,
    new_kv,
    cycle_pos,
    out_weight,
    norm_gain,
    route_logits,
    expert_ids,
    expert_in,
    expert_out,
):
    devices = lax.axis_size("tensor")
    hidden, cache = layer(
        devices,
        queries,
        hidden_in,
        norm_gain.reshape(1, -1),
        route_logits,
        expert_ids,
        new_kv,
        cycle_pos,
        kv_cache,
        (out_weight, expert_in, expert_out),
    )
    return store(hidden, cache)


def solution(mesh):
    return jax.shard_map(
        on_device,
        mesh=mesh,
        in_specs=(
            P(("group", "tensor"), None),
            P(("group", "tensor"), None),
            P(("group", "tensor"), None, None),
            P(("group", "tensor"), None),
            P("group"),
            P("tensor", None),
            P(),
            P(("group", "tensor"), None),
            P(("group", "tensor"), None),
            P("tensor", None, None),
            P("tensor", None, None),
        ),
        out_specs=(P(("group", "tensor"), None), P(("group", "tensor"), None, None)),
        check_vma=False,
    )
```

```python
import functools
import math

import jax
import jax.numpy as jnp
from jax import lax
from jax.experimental import pallas as pl
from jax.experimental.pallas import tpu as pltpu
from jax.sharding import PartitionSpec as P

HD = 128
SINK = 4
MESH = pl.DeviceIdType.MESH


def wait_bytes(ref, sem):
    pltpu.make_async_copy(ref, ref, sem).wait()


CHUNKS = (4, 1)
PIECES = (1, 2)
HALVED = ((1,), (1,), (1,))


def layer_kernel(
    n,
    queries_hbm,
    hidden_hbm,
    gain_hbm,
    logits_hbm,
    ids_hbm,
    new_kv_hbm,
    cycle_hbm,
    kv_cache,
    out_weight,
    expert_in,
    expert_out,
    hidden_out,
    cache,
    queries,
    hidden_in,
    norm_gain,
    route_logits,
    expert_ids,
    new_kv,
    cycle_pos,
    w_proj,
    w_in,
    w_out,
    query_rows,
    score_rows,
    out_rows,
    by_head,
    heads,
    chip_out_a,
    chip_out_b,
    chip_in_a,
    chip_in_b,
    mid,
    gathered,
    gathered_last,
    joined,
    act,
    load_sem,
    swap_send,
    swap_recv,
    head_send,
    head_recv,
    chip_send_a,
    chip_send_b,
    chip_recv_a,
    chip_recv_b,
    ag_send,
    ag_recv,
    far_in_a,
    far_in_b,
    far_out_a,
    far_out_b,
    far_recv_a,
    far_recv_b,
    cross_recv,
):
    me = lax.axis_index("tensor")
    chips = n // 2
    chip, core = me // 2, me % 2
    partner = chip * 2 + (1 - core)
    tokens, width = hidden_in.shape
    ff = w_out.shape[1]
    half = chips * tokens
    parts = [width // count for count in CHUNKS]
    part = parts[0]
    chip_out, chip_in = (chip_out_a, chip_out_b), (chip_in_a, chip_in_b)
    far_in, far_out, far_recv = (far_in_a, far_in_b), (far_out_a, far_out_b), (far_recv_a, far_recv_b)
    chip_send, chip_recv = (chip_send_a, chip_send_b), (chip_recv_a, chip_recv_b)
    f32, bf16 = jnp.float32, jnp.bfloat16

    halved_gather, *halved_sum = HALVED
    near_count = chips // 2
    base = chip // near_count * near_count
    mirror = lax.rem(chip + near_count, chips)

    def peer(step):
        return lax.rem(chip + step, chips)

    def facing(step):
        return lax.bitwise_xor(chip, chips - step) if chips & (chips - 1) == 0 else peer(step)

    def near(step):
        return base + lax.rem(chip - base + step, near_count)

    def of_cores(cores, first, second):
        for number in range(2):
            pl.when(core == number)(first if number in cores else second)

    def send_to(to, src, dst, send_sem, recv_sem):
        pltpu.make_async_remote_copy(
            src_ref=src,
            dst_ref=dst,
            send_sem=send_sem,
            recv_sem=recv_sem,
            device_id={"tensor": to * 2 + core},
            device_id_type=MESH,
        ).start()

    barrier = pltpu.get_barrier_semaphore()
    pl.semaphore_signal(barrier, inc=1, device_id={"tensor": partner}, device_id_type=MESH)

    @pl.loop(1, chips)
    def _(step):
        pl.semaphore_signal(
            barrier, inc=1, device_id={"tensor": peer(step) * 2 + core}, device_id_type=MESH
        )

    pairs = (
        (kv_cache, cache),
        (queries_hbm, queries),
        (new_kv_hbm, new_kv),
        (cycle_hbm, cycle_pos),
        (logits_hbm, route_logits),
        (ids_hbm, expert_ids),
        (hidden_hbm, hidden_in),
        (gain_hbm, norm_gain),
        (out_weight, w_proj.at[core]),
        (expert_in.at[0], w_in.at[core]),
        (expert_out.at[0], w_out.at[core]),
    )
    loads = [pltpu.make_async_copy(a, b, load_sem.at[i]) for i, (a, b) in enumerate(pairs)]
    for load in loads[:8]:
        load.start()

    def piece_of(c):
        return pl.ds(c * part, part)

    swapped = [
        (out_weight.at[:, piece_of(c)], w_proj.at[core, :, piece_of(c)]) for c in range(CHUNKS[0])
    ]
    swapped += [
        (expert_in.at[0, piece_of(c)], w_in.at[core, piece_of(c)]) for c in range(CHUNKS[0])
    ]
    for p in range(PIECES[1]):
        columns = pl.ds(p * (width // PIECES[1]), width // PIECES[1])
        swapped += [(expert_out.at[0, :, columns], w_out.at[core, :, columns])]
    swaps = [
        pltpu.make_async_remote_copy(
            src_ref=a,
            dst_ref=b,
            send_sem=swap_send.at[i],
            recv_sem=swap_recv.at[i],
            device_id={"tensor": partner},
            device_id_type=MESH,
        )
        for i, (a, b) in enumerate(swapped)
    ]

    rows_here = cache.shape[0]
    kv_heads = rows_here // tokens
    per_kv = queries.shape[1] // HD
    loads[1].wait()
    for h in range(per_kv):
        query_rows[h * rows_here : (h + 1) * rows_here, :] = queries[
            :, h * HD : (h + 1) * HD
        ].astype(f32)
    for load in (loads[0], loads[2], loads[3]):
        load.wait()
    for load in loads[8:]:
        load.start()
    slot_ids = lax.broadcasted_iota(jnp.int32, cache.shape[1:], 0)
    for t in range(tokens):
        written = slot_ids == cycle_pos[me * tokens + t] + SINK
        for r in range(t * kv_heads, (t + 1) * kv_heads):
            cache[r] = jnp.where(
                written, new_kv[r : r + 1, :].astype(f32), cache[r].astype(f32)
            ).astype(bf16)
    for r in range(rows_here):
        query = query_rows[pl.ds(r, per_kv, stride=rows_here), :].astype(bf16)
        score_rows[r * per_kv : (r + 1) * per_kv, :] = lax.dot_general(
            query,
            cache[r, :, :HD],
            (((1,), (1,)), ((), ())),
            preferred_element_type=f32,
        )
    scores = score_rows[...] / math.sqrt(HD)
    powers = jnp.exp(scores - jnp.max(scores, axis=-1, keepdims=True))
    score_rows[...] = powers / jnp.sum(powers, axis=-1, keepdims=True)
    for r in range(rows_here):
        probs = score_rows[r * per_kv : (r + 1) * per_kv, :].astype(bf16)
        first = (r % kv_heads) * per_kv * tokens + r // kv_heads
        out_rows[pl.ds(first, per_kv, stride=tokens), :] = jnp.dot(
            probs, cache[r, :, HD:], preferred_element_type=f32
        )
    by_head[...] = out_rows[...].reshape(by_head.shape).astype(bf16)

    for r in range(2):

        def clear(r=r):
            @pl.loop(1, near_count)
            def _(step):
                slot = lax.rem(near(step) + near_count, chips)
                for c in range(CHUNKS[r]):
                    chip_in[r][c, slot] = jnp.zeros((tokens, parts[r]), bf16)

        of_cores(halved_sum[r], clear, lambda: None)
    pl.semaphore_wait(barrier, chips)
    swaps[0].start()

    @pl.loop(1, chips)
    def _(step):
        to = facing(step)
        pltpu.make_async_remote_copy(
            src_ref=by_head.at[to],
            dst_ref=heads.at[chip],
            send_sem=head_send,
            recv_sem=head_recv,
            device_id={"tensor": to * 2 + core},
            device_id_type=MESH,
        ).start()

    for swap in swaps[1:]:
        swap.start()
    heads[chip] = by_head[chip]

    for load in loads[4:8]:
        load.wait()
    logits = route_logits[...]
    top = logits.shape[1]
    powers = jnp.exp(logits - jnp.max(logits, axis=-1, keepdims=True))
    gate = (powers / jnp.sum(powers, axis=-1, keepdims=True)).astype(bf16).astype(f32)
    pad = gathered_last.shape[2] - part
    lanes = lax.broadcasted_iota(jnp.int32, (tokens, pad), 1)
    ids = expert_ids[...]
    table = jnp.zeros((tokens, pad), f32)
    for j in range(top):
        table = table + jnp.where(lanes == ids[:, j : j + 1], gate[:, j : j + 1], 0.0)

    def block(c):
        return gathered_last if c == CHUNKS[0] - 1 else gathered.at[c]

    def rows_of(ref, lo, hi):
        return ref[:, :, lo:hi].astype(f32).reshape(half, hi - lo)

    def cut(r, p):
        step = parts[r] // PIECES[r]
        return pl.ds(p * step, step)

    def put(r, c, p, rows):
        columns = cut(r, p)
        chip_out[r][c, :, :, columns] = rows.reshape(chips, tokens, columns.size).astype(bf16)

        def halved():
            @pl.loop(1, near_count)
            def _(step):
                to = near(step)
                send_to(
                    to,
                    chip_out[r].at[c, lax.rem(to + near_count, chips), :, columns],
                    far_in[r].at[c, chip - base, :, columns],
                    chip_send[r].at[c],
                    far_recv[r].at[c, p],
                )

        of_cores(halved_sum[r], halved, lambda: None)

    def scatter(r, c):
        out, sent = chip_out[r].at[c], chip_send[r].at[c]

        def block_to(to):
            send_to(to, out.at[to], chip_in[r].at[c, chip], sent, chip_recv[r].at[c])

        def direct():
            @pl.loop(1, chips)
            def _(step):
                block_to(facing(step) if r == 0 else peer(step))

        def halved():
            @pl.loop(1, near_count)
            def _(step):
                block_to(near(step))

        of_cores(halved_sum[r], halved, direct)
        chip_in[r][c, chip] = chip_out[r][c, chip]

    def cross(r, c):
        def halved():
            far_in[r][c, chip - base] = chip_out[r][c, mirror]
            for p in range(PIECES[r]):
                columns = cut(r, p)
                wait_bytes(
                    far_in[r].at[c, pl.ds(0, near_count - 1), :, columns], far_recv[r].at[c, p]
                )
                far_out[r][c, :, columns] = jnp.sum(
                    far_in[r][c, :, :, columns].astype(f32), axis=0
                ).astype(bf16)
                send_to(
                    mirror,
                    far_out[r].at[c, :, columns],
                    chip_in[r].at[c, chip, :, columns],
                    chip_send[r].at[c],
                    chip_recv[r].at[c],
                )

        of_cores(halved_sum[r], halved, lambda: None)

    def collect(r, c):
        of_cores(
            halved_sum[r],
            lambda: wait_bytes(chip_in[r].at[c, pl.ds(0, near_count)], chip_recv[r].at[c]),
            lambda: wait_bytes(chip_in[r].at[c, pl.ds(0, chips - 1)], chip_recv[r].at[c]),
        )
        return jnp.sum(chip_in[r][c].astype(f32), axis=0)

    wait_bytes(heads.at[pl.ds(0, chips - 1)], head_recv)
    arrived = heads[...].astype(f32)
    head_all = jnp.concatenate(
        [arrived[:, h].reshape(half, HD) for h in range(heads.shape[1])], axis=-1
    ).astype(bf16)
    loads[8].wait()
    depth = w_proj.shape[1]
    for c in range(CHUNKS[0]):
        columns = slice(c * part, (c + 1) * part)
        swaps[c].wait_recv()
        rows = jnp.dot(
            head_all,
            w_proj[:, :, columns].reshape(2 * depth, part),
            preferred_element_type=f32,
        )
        put(0, c, 0, rows)
        scatter(0, c)

    for c in range(CHUNKS[0]):
        cross(0, c)
    squares = jnp.zeros((tokens, 1), f32)
    for c in range(CHUNKS[0]):
        columns = slice(c * part, (c + 1) * part)
        wide = (hidden_in[:, columns].astype(f32) + collect(0, c)).astype(bf16).astype(f32)
        mid[:, columns] = wide
        squares = squares + jnp.sum(wide * wide, axis=-1, keepdims=True)
        to_send = block(c)
        to_send[chip, :, :part] = (wide * norm_gain[:, columns]).astype(bf16)
        if c == CHUNKS[0] - 1:
            scale = lax.rsqrt(squares / width + 1e-06)
            high = scale.astype(bf16).astype(f32)
            info = jnp.where(lanes == n, high, jnp.where(lanes == n + 1, scale - high, table))
            to_send[chip, :, part:] = info.astype(bf16)

        def direct(c=c, mine=to_send.at[chip]):
            @pl.loop(1, chips)
            def _(step):
                send_to(facing(step), mine, mine, ag_send.at[c], ag_recv.at[c])

        def halved(c=c, mine=to_send.at[chip]):
            send_to(mirror, mine, mine, ag_send.at[c], cross_recv.at[c])

            @pl.loop(1, near_count)
            def _(step):
                send_to(near(step), mine, mine, ag_send.at[c], ag_recv.at[c])

        of_cores(halved_gather, halved, direct)

    def forward(c):
        def halved():
            theirs = block(c).at[mirror]
            wait_bytes(theirs, cross_recv.at[c])

            @pl.loop(1, near_count)
            def _(step):
                send_to(near(step), theirs, theirs, ag_send.at[c], ag_recv.at[c])

        of_cores(halved_gather, halved, lambda: None)

    for c in range(CHUNKS[0]):
        forward(c)

    piece = 256

    def product(rows, k, c, lo):
        term = jnp.dot(
            rows,
            w_in[k, c * part : (c + 1) * part, lo : lo + piece],
            preferred_element_type=f32,
        )
        return term if c == 0 else joined[k, :, lo : lo + piece] + term

    last = CHUNKS[0] - 1
    loads[9].wait()
    for c in range(CHUNKS[0]):
        swaps[CHUNKS[0] + c].wait_recv()
        of_cores(
            halved_gather,
            lambda c=c: wait_bytes(block(c).at[pl.ds(0, chips - 2)], ag_recv.at[c]),
            lambda c=c: wait_bytes(block(c).at[pl.ds(0, chips - 1)], ag_recv.at[c]),
        )
        rows = rows_of(block(c), 0, part).astype(bf16)
        if c < last:
            for k in range(2):
                for lo in range(0, 2 * ff, piece):
                    joined[k, :, lo : lo + piece] = product(rows, k, c, lo)
    lane = lax.broadcasted_iota(jnp.int32, (half, pad), 1)
    info = rows_of(block(last), part, part + pad)
    scale = jnp.sum(
        jnp.where((lane == n) | (lane == n + 1), info, 0.0), axis=-1, keepdims=True
    )
    for k in range(2):
        share = jnp.sum(jnp.where(lane == chip * 2 + k, info, 0.0), axis=-1, keepdims=True)
        for lo in range(0, ff, piece):
            gate_part = product(rows, k, last, lo) * scale
            up_part = product(rows, k, last, ff + lo) * scale
            act[:, k * ff + lo : k * ff + lo + piece] = (
                gate_part / (1.0 + jnp.exp(-gate_part)) * up_part * share
            ).astype(bf16)
    loads[10].wait()
    for c in range(CHUNKS[1]):
        for p in range(PIECES[1]):
            swaps[2 * CHUNKS[0] + p].wait_recv()
            columns = cut(1, p)
            low = c * parts[1] + columns.start
            rows = jnp.dot(
                act[...],
                w_out[:, :, low : low + columns.size].reshape(2 * ff, columns.size),
                preferred_element_type=f32,
            )
            put(1, c, p, rows)
        scatter(1, c)
    for c in range(CHUNKS[1]):
        cross(1, c)
    for c in range(CHUNKS[1]):
        columns = slice(c * parts[1], (c + 1) * parts[1])
        hidden_out[:, columns] = (mid[:, columns] + collect(1, c)).astype(bf16)

    wait_bytes(heads.at[pl.ds(0, chips - 1)], head_send)
    for swap in swaps:
        swap.wait_send()
    for r in range(2):
        for c in range(CHUNKS[r]):
            wait_bytes(chip_out[r].at[c, pl.ds(0, chips - 1)], chip_send[r].at[c])
    for c in range(CHUNKS[0]):
        wait_bytes(block(c).at[pl.ds(0, chips - 1)], ag_send.at[c])


def layer(n, queries, hidden_in, norm_gain, route_logits, expert_ids, new_kv, cycle_pos, kv_cache, weights):
    tokens, width = hidden_in.shape
    out_weight, expert_in, expert_out = weights
    ff = expert_out.shape[1]
    chips = n // 2
    parts = [width // count for count in CHUNKS]
    part = parts[0]
    both = tuple(zip(CHUNKS, parts))
    pad = -(-(n + 2) // 128) * 128
    rows_here, slots, _ = kv_cache.shape
    heads_all = rows_here // tokens * (queries.shape[1] // HD)
    exchange = (chips, heads_all // chips, tokens, HD)
    bf16, f32 = jnp.bfloat16, jnp.float32
    hbm = pl.BlockSpec(memory_space=pl.ANY)
    vmem = pl.BlockSpec(memory_space=pltpu.VMEM)
    dma = pltpu.SemaphoreType.DMA
    small = (queries, hidden_in, norm_gain, route_logits, expert_ids, new_kv)
    return pl.pallas_call(
        functools.partial(layer_kernel, n),
        out_shape=(
            pltpu.VMEM((tokens, width), bf16),
            pltpu.VMEM(kv_cache.shape, bf16),
        ),
        in_specs=[hbm] * 11,
        out_specs=(vmem, vmem),
        scratch_shapes=[pltpu.VMEM(a.shape, a.dtype) for a in small]
        + [
            pltpu.SMEM(cycle_pos.shape, cycle_pos.dtype),
            pltpu.VMEM((2,) + out_weight.shape, bf16),
            pltpu.VMEM((2,) + expert_in.shape[1:], bf16),
            pltpu.VMEM((2,) + expert_out.shape[1:], bf16),
            pltpu.VMEM((heads_all * tokens, HD), f32),
            pltpu.VMEM((heads_all * tokens, slots), f32),
            pltpu.VMEM((heads_all * tokens, HD), f32),
            pltpu.VMEM(exchange, bf16),
            pltpu.VMEM(exchange, bf16),
            *[pltpu.VMEM((c, chips, tokens, p), bf16) for c, p in both],
            *[pltpu.VMEM((c, chips, tokens, p), bf16) for c, p in both],
            pltpu.VMEM((tokens, width), f32),
            pltpu.VMEM((CHUNKS[0] - 1, chips, tokens, part), bf16),
            pltpu.VMEM((chips, tokens, part + pad), bf16),
            pltpu.VMEM((2, chips * tokens, 2 * ff), f32),
            pltpu.VMEM((chips * tokens, 2 * ff), bf16),
            dma((11,)),
            dma((2 * CHUNKS[0] + PIECES[1],)),
            dma((2 * CHUNKS[0] + PIECES[1],)),
            dma,
            dma,
            *[dma((c,)) for c in CHUNKS],
            *[dma((c,)) for c in CHUNKS],
            dma((CHUNKS[0],)),
            dma((CHUNKS[0],)),
            *[pltpu.VMEM((c, chips // 2, tokens, p), bf16) for c, p in both],
            *[pltpu.VMEM((c, tokens, p), bf16) for c, p in both],
            *[dma((c, p)) for c, p in zip(CHUNKS, PIECES)],
            dma((CHUNKS[0],)),
        ],
        compiler_params=pltpu.CompilerParams(
            collective_id=0, has_side_effects=True, vmem_limit_bytes=56 * 1024 * 1024
        ),
        name="layer",
    )(
        queries,
        hidden_in,
        norm_gain,
        route_logits,
        expert_ids,
        new_kv,
        cycle_pos,
        kv_cache,
        out_weight,
        expert_in,
        expert_out,
    )


def store_kernel(hidden, cache, hidden_out, new_cache, sems):
    copies = (
        pltpu.make_async_copy(cache, new_cache, sems.at[1]),
        pltpu.make_async_copy(hidden, hidden_out, sems.at[0]),
    )
    for copy in copies:
        copy.start()
    for copy in copies:
        copy.wait()


def store(hidden, cache):
    anywhere = pl.BlockSpec(memory_space=pl.ANY)
    return pl.pallas_call(
        store_kernel,
        out_shape=tuple(jax.ShapeDtypeStruct(a.shape, a.dtype) for a in (hidden, cache)),
        in_specs=[pl.BlockSpec(memory_space=pltpu.VMEM)] * 2,
        out_specs=(anywhere,) * 2,
        scratch_shapes=[pltpu.SemaphoreType.DMA((2,))],
        name="store",
    )(*(pltpu.with_memory_space_constraint(a, pltpu.VMEM) for a in (hidden, cache)))


def on_device(
    hidden_in,
    queries,
    kv_cache,
    new_kv,
    cycle_pos,
    out_weight,
    norm_gain,
    route_logits,
    expert_ids,
    expert_in,
    expert_out,
):
    devices = lax.axis_size("tensor")
    hidden, cache = layer(
        devices,
        queries,
        hidden_in,
        norm_gain.reshape(1, -1),
        route_logits,
        expert_ids,
        new_kv,
        cycle_pos,
        kv_cache,
        (out_weight, expert_in, expert_out),
    )
    return store(hidden, cache)


def solution(mesh):
    return jax.shard_map(
        on_device,
        mesh=mesh,
        in_specs=(
            P(("group", "tensor"), None),
            P(("group", "tensor"), None),
            P(("group", "tensor"), None, None),
            P(("group", "tensor"), None),
            P("group"),
            P("tensor", None),
            P(),
            P(("group", "tensor"), None),
            P(("group", "tensor"), None),
            P("tensor", None, None),
            P("tensor", None, None),
        ),
        out_specs=(P(("group", "tensor"), None), P(("group", "tensor"), None, None)),
        check_vma=False,
    )
```

```python
import functools
import math

import jax
import jax.numpy as jnp
from jax import lax
from jax.experimental import pallas as pl
from jax.experimental.pallas import tpu as pltpu
from jax.sharding import PartitionSpec as P

HD = 128
SINK = 4
MESH = pl.DeviceIdType.MESH


def wait_bytes(ref, sem):
    pltpu.make_async_copy(ref, ref, sem).wait()


CHUNKS = (4, 1)
PIECES = (1, 2)
HALVED = ((1,), (1,), (1,))


def layer_kernel(
    n,
    queries_hbm,
    hidden_hbm,
    gain_hbm,
    logits_hbm,
    ids_hbm,
    new_kv_hbm,
    cycle_hbm,
    kv_cache,
    out_weight,
    expert_in,
    expert_out,
    hidden_out,
    cache,
    queries,
    hidden_in,
    norm_gain,
    route_logits,
    expert_ids,
    new_kv,
    cycle_pos,
    w_proj,
    w_in,
    w_out,
    query_rows,
    score_rows,
    out_rows,
    by_head,
    heads,
    chip_out_a,
    chip_out_b,
    chip_in_a,
    chip_in_b,
    mid,
    gathered,
    gathered_last,
    joined,
    act,
    load_sem,
    swap_send,
    swap_recv,
    head_send,
    head_recv,
    chip_send_a,
    chip_send_b,
    chip_recv_a,
    chip_recv_b,
    ag_send,
    ag_recv,
    far_in_a,
    far_in_b,
    far_out_a,
    far_out_b,
    far_recv_a,
    far_recv_b,
    cross_recv,
):
    me = lax.axis_index("tensor")
    chips = n // 2
    chip, core = me // 2, me % 2
    partner = chip * 2 + (1 - core)
    tokens, width = hidden_in.shape
    ff = w_out.shape[1]
    half = chips * tokens
    parts = [width // count for count in CHUNKS]
    part = parts[0]
    chip_out, chip_in = (chip_out_a, chip_out_b), (chip_in_a, chip_in_b)
    far_in, far_out, far_recv = (far_in_a, far_in_b), (far_out_a, far_out_b), (far_recv_a, far_recv_b)
    chip_send, chip_recv = (chip_send_a, chip_send_b), (chip_recv_a, chip_recv_b)
    f32, bf16 = jnp.float32, jnp.bfloat16

    halved_gather, *halved_sum = HALVED
    near_count = chips // 2
    base = chip // near_count * near_count
    mirror = lax.rem(chip + near_count, chips)

    def peer(step):
        return lax.rem(chip + step, chips)

    def facing(step):
        return lax.bitwise_xor(chip, chips - step) if chips & (chips - 1) == 0 else peer(step)

    def near(step):
        return base + lax.rem(chip - base + step, near_count)

    def of_cores(cores, first, second):
        for number in range(2):
            pl.when(core == number)(first if number in cores else second)

    def send_to(to, src, dst, send_sem, recv_sem):
        pltpu.make_async_remote_copy(
            src_ref=src,
            dst_ref=dst,
            send_sem=send_sem,
            recv_sem=recv_sem,
            device_id={"tensor": to * 2 + core},
            device_id_type=MESH,
        ).start()

    barrier = pltpu.get_barrier_semaphore()
    pl.semaphore_signal(barrier, inc=1, device_id={"tensor": partner}, device_id_type=MESH)

    @pl.loop(1, chips)
    def _(step):
        pl.semaphore_signal(
            barrier, inc=1, device_id={"tensor": peer(step) * 2 + core}, device_id_type=MESH
        )

    pairs = (
        (kv_cache, cache),
        (queries_hbm, queries),
        (new_kv_hbm, new_kv),
        (cycle_hbm, cycle_pos),
        (logits_hbm, route_logits),
        (ids_hbm, expert_ids),
        (hidden_hbm, hidden_in),
        (gain_hbm, norm_gain),
        (out_weight, w_proj.at[core]),
        (expert_in.at[0], w_in.at[core]),
        (expert_out.at[0], w_out.at[core]),
    )
    loads = [pltpu.make_async_copy(a, b, load_sem.at[i]) for i, (a, b) in enumerate(pairs)]
    for load in loads[:8]:
        load.start()

    def piece_of(c):
        return pl.ds(c * part, part)

    swapped = [
        (out_weight.at[:, piece_of(c)], w_proj.at[core, :, piece_of(c)]) for c in range(CHUNKS[0])
    ]
    swapped += [
        (expert_in.at[0, piece_of(c)], w_in.at[core, piece_of(c)]) for c in range(CHUNKS[0])
    ]
    for p in range(PIECES[1]):
        columns = pl.ds(p * (width // PIECES[1]), width // PIECES[1])
        swapped += [(expert_out.at[0, :, columns], w_out.at[core, :, columns])]
    swaps = [
        pltpu.make_async_remote_copy(
            src_ref=a,
            dst_ref=b,
            send_sem=swap_send.at[i],
            recv_sem=swap_recv.at[i],
            device_id={"tensor": partner},
            device_id_type=MESH,
        )
        for i, (a, b) in enumerate(swapped)
    ]

    rows_here = cache.shape[0]
    kv_heads = rows_here // tokens
    per_kv = queries.shape[1] // HD
    loads[1].wait()
    for h in range(per_kv):
        query_rows[h * rows_here : (h + 1) * rows_here, :] = queries[
            :, h * HD : (h + 1) * HD
        ].astype(f32)
    for load in (loads[0], loads[2], loads[3]):
        load.wait()
    for load in loads[8:]:
        load.start()
    slot_ids = lax.broadcasted_iota(jnp.int32, cache.shape[1:], 0)
    for t in range(tokens):
        written = slot_ids == cycle_pos[me * tokens + t] + SINK
        for r in range(t * kv_heads, (t + 1) * kv_heads):
            cache[r] = jnp.where(
                written, new_kv[r : r + 1, :].astype(f32), cache[r].astype(f32)
            ).astype(bf16)
    for r in range(rows_here):
        query = query_rows[pl.ds(r, per_kv, stride=rows_here), :].astype(bf16)
        score_rows[r * per_kv : (r + 1) * per_kv, :] = lax.dot_general(
            query,
            cache[r, :, :HD],
            (((1,), (1,)), ((), ())),
            preferred_element_type=f32,
        )
    scores = score_rows[...] / math.sqrt(HD)
    powers = jnp.exp(scores - jnp.max(scores, axis=-1, keepdims=True))
    score_rows[...] = powers / jnp.sum(powers, axis=-1, keepdims=True)
    for r in range(rows_here):
        probs = score_rows[r * per_kv : (r + 1) * per_kv, :].astype(bf16)
        first = (r % kv_heads) * per_kv * tokens + r // kv_heads
        out_rows[pl.ds(first, per_kv, stride=tokens), :] = jnp.dot(
            probs, cache[r, :, HD:], preferred_element_type=f32
        )
    by_head[...] = out_rows[...].reshape(by_head.shape).astype(bf16)

    for r in range(2):

        def clear(r=r):
            @pl.loop(1, near_count, unroll=True)
            def _(step):
                slot = lax.rem(near(step) + near_count, chips)
                for c in range(CHUNKS[r]):
                    chip_in[r][c, slot] = jnp.zeros((tokens, parts[r]), bf16)

        of_cores(halved_sum[r], clear, lambda: None)
    pl.semaphore_wait(barrier, chips)
    swaps[0].start()

    @pl.loop(1, chips)
    def _(step):
        to = facing(step)
        pltpu.make_async_remote_copy(
            src_ref=by_head.at[to],
            dst_ref=heads.at[chip],
            send_sem=head_send,
            recv_sem=head_recv,
            device_id={"tensor": to * 2 + core},
            device_id_type=MESH,
        ).start()

    for swap in swaps[1:]:
        swap.start()
    heads[chip] = by_head[chip]

    for load in loads[4:8]:
        load.wait()
    logits = route_logits[...]
    top = logits.shape[1]
    powers = jnp.exp(logits - jnp.max(logits, axis=-1, keepdims=True))
    gate = (powers / jnp.sum(powers, axis=-1, keepdims=True)).astype(bf16).astype(f32)
    pad = gathered_last.shape[2] - part
    lanes = lax.broadcasted_iota(jnp.int32, (tokens, pad), 1)
    ids = expert_ids[...]
    table = jnp.zeros((tokens, pad), f32)
    for j in range(top):
        table = table + jnp.where(lanes == ids[:, j : j + 1], gate[:, j : j + 1], 0.0)

    def block(c):
        return gathered_last if c == CHUNKS[0] - 1 else gathered.at[c]

    def rows_of(ref, lo, hi):
        return ref[:, :, lo:hi].astype(f32).reshape(half, hi - lo)

    def cut(r, p):
        step = parts[r] // PIECES[r]
        return pl.ds(p * step, step)

    def put(r, c, p, rows):
        columns = cut(r, p)
        chip_out[r][c, :, :, columns] = rows.reshape(chips, tokens, columns.size).astype(bf16)

        def halved():
            @pl.loop(1, near_count, unroll=True)
            def _(step):
                to = near(step)
                send_to(
                    to,
                    chip_out[r].at[c, lax.rem(to + near_count, chips), :, columns],
                    far_in[r].at[c, chip - base, :, columns],
                    chip_send[r].at[c],
                    far_recv[r].at[c, p],
                )

        of_cores(halved_sum[r], halved, lambda: None)

    def scatter(r, c):
        out, sent = chip_out[r].at[c], chip_send[r].at[c]

        def block_to(to):
            send_to(to, out.at[to], chip_in[r].at[c, chip], sent, chip_recv[r].at[c])

        def direct():
            @pl.loop(1, chips)
            def _(step):
                block_to(facing(step) if r == 0 else peer(step))

        def halved():
            @pl.loop(1, near_count, unroll=True)
            def _(step):
                block_to(near(step))

        of_cores(halved_sum[r], halved, direct)
        chip_in[r][c, chip] = chip_out[r][c, chip]

    def cross(r, c):
        def halved():
            far_in[r][c, chip - base] = chip_out[r][c, mirror]
            for p in range(PIECES[r]):
                columns = cut(r, p)
                wait_bytes(
                    far_in[r].at[c, pl.ds(0, near_count - 1), :, columns], far_recv[r].at[c, p]
                )
                far_out[r][c, :, columns] = jnp.sum(
                    far_in[r][c, :, :, columns].astype(f32), axis=0
                ).astype(bf16)
                send_to(
                    mirror,
                    far_out[r].at[c, :, columns],
                    chip_in[r].at[c, chip, :, columns],
                    chip_send[r].at[c],
                    chip_recv[r].at[c],
                )

        of_cores(halved_sum[r], halved, lambda: None)

    def collect(r, c):
        of_cores(
            halved_sum[r],
            lambda: wait_bytes(chip_in[r].at[c, pl.ds(0, near_count)], chip_recv[r].at[c]),
            lambda: wait_bytes(chip_in[r].at[c, pl.ds(0, chips - 1)], chip_recv[r].at[c]),
        )
        return jnp.sum(chip_in[r][c].astype(f32), axis=0)

    wait_bytes(heads.at[pl.ds(0, chips - 1)], head_recv)
    arrived = heads[...].astype(f32)
    head_all = jnp.concatenate(
        [arrived[:, h].reshape(half, HD) for h in range(heads.shape[1])], axis=-1
    ).astype(bf16)
    loads[8].wait()
    depth = w_proj.shape[1]
    for c in range(CHUNKS[0]):
        columns = slice(c * part, (c + 1) * part)
        swaps[c].wait_recv()
        rows = jnp.dot(
            head_all,
            w_proj[:, :, columns].reshape(2 * depth, part),
            preferred_element_type=f32,
        )
        put(0, c, 0, rows)
        scatter(0, c)

    for c in range(CHUNKS[0]):
        cross(0, c)
    squares = jnp.zeros((tokens, 1), f32)
    for c in range(CHUNKS[0]):
        columns = slice(c * part, (c + 1) * part)
        wide = (hidden_in[:, columns].astype(f32) + collect(0, c)).astype(bf16).astype(f32)
        mid[:, columns] = wide
        squares = squares + jnp.sum(wide * wide, axis=-1, keepdims=True)
        to_send = block(c)
        to_send[chip, :, :part] = (wide * norm_gain[:, columns]).astype(bf16)
        if c == CHUNKS[0] - 1:
            scale = lax.rsqrt(squares / width + 1e-06)
            high = scale.astype(bf16).astype(f32)
            info = jnp.where(lanes == n, high, jnp.where(lanes == n + 1, scale - high, table))
            to_send[chip, :, part:] = info.astype(bf16)

        def direct(c=c, mine=to_send.at[chip]):
            @pl.loop(1, chips)
            def _(step):
                send_to(facing(step), mine, mine, ag_send.at[c], ag_recv.at[c])

        def halved(c=c, mine=to_send.at[chip]):
            send_to(mirror, mine, mine, ag_send.at[c], cross_recv.at[c])

            @pl.loop(1, near_count, unroll=True)
            def _(step):
                send_to(near(step), mine, mine, ag_send.at[c], ag_recv.at[c])

        of_cores(halved_gather, halved, direct)

    def forward(c):
        def halved():
            theirs = block(c).at[mirror]
            wait_bytes(theirs, cross_recv.at[c])

            @pl.loop(1, near_count, unroll=True)
            def _(step):
                send_to(near(step), theirs, theirs, ag_send.at[c], ag_recv.at[c])

        of_cores(halved_gather, halved, lambda: None)

    for c in range(CHUNKS[0]):
        forward(c)

    piece = 256

    def product(rows, k, c, lo):
        term = jnp.dot(
            rows,
            w_in[k, c * part : (c + 1) * part, lo : lo + piece],
            preferred_element_type=f32,
        )
        return term if c == 0 else joined[k, :, lo : lo + piece] + term

    last = CHUNKS[0] - 1
    loads[9].wait()
    for c in range(CHUNKS[0]):
        swaps[CHUNKS[0] + c].wait_recv()
        of_cores(
            halved_gather,
            lambda c=c: wait_bytes(block(c).at[pl.ds(0, chips - 2)], ag_recv.at[c]),
            lambda c=c: wait_bytes(block(c).at[pl.ds(0, chips - 1)], ag_recv.at[c]),
        )
        rows = rows_of(block(c), 0, part).astype(bf16)
        if c < last:
            for k in range(2):
                for lo in range(0, 2 * ff, piece):
                    joined[k, :, lo : lo + piece] = product(rows, k, c, lo)
    lane = lax.broadcasted_iota(jnp.int32, (half, pad), 1)
    info = rows_of(block(last), part, part + pad)
    scale = jnp.sum(
        jnp.where((lane == n) | (lane == n + 1), info, 0.0), axis=-1, keepdims=True
    )
    for k in range(2):
        share = jnp.sum(jnp.where(lane == chip * 2 + k, info, 0.0), axis=-1, keepdims=True)
        for lo in range(0, ff, piece):
            gate_part = product(rows, k, last, lo) * scale
            up_part = product(rows, k, last, ff + lo) * scale
            act[:, k * ff + lo : k * ff + lo + piece] = (
                gate_part / (1.0 + jnp.exp(-gate_part)) * up_part * share
            ).astype(bf16)
    loads[10].wait()
    for c in range(CHUNKS[1]):
        for p in range(PIECES[1]):
            swaps[2 * CHUNKS[0] + p].wait_recv()
            columns = cut(1, p)
            low = c * parts[1] + columns.start
            rows = jnp.dot(
                act[...],
                w_out[:, :, low : low + columns.size].reshape(2 * ff, columns.size),
                preferred_element_type=f32,
            )
            put(1, c, p, rows)
        scatter(1, c)
    for c in range(CHUNKS[1]):
        cross(1, c)
    for c in range(CHUNKS[1]):
        columns = slice(c * parts[1], (c + 1) * parts[1])
        hidden_out[:, columns] = (mid[:, columns] + collect(1, c)).astype(bf16)

    wait_bytes(heads.at[pl.ds(0, chips - 1)], head_send)
    for swap in swaps:
        swap.wait_send()
    for r in range(2):
        for c in range(CHUNKS[r]):
            wait_bytes(chip_out[r].at[c, pl.ds(0, chips - 1)], chip_send[r].at[c])
    for c in range(CHUNKS[0]):
        wait_bytes(block(c).at[pl.ds(0, chips - 1)], ag_send.at[c])


def layer(n, queries, hidden_in, norm_gain, route_logits, expert_ids, new_kv, cycle_pos, kv_cache, weights):
    tokens, width = hidden_in.shape
    out_weight, expert_in, expert_out = weights
    ff = expert_out.shape[1]
    chips = n // 2
    parts = [width // count for count in CHUNKS]
    part = parts[0]
    both = tuple(zip(CHUNKS, parts))
    pad = -(-(n + 2) // 128) * 128
    rows_here, slots, _ = kv_cache.shape
    heads_all = rows_here // tokens * (queries.shape[1] // HD)
    exchange = (chips, heads_all // chips, tokens, HD)
    bf16, f32 = jnp.bfloat16, jnp.float32
    hbm = pl.BlockSpec(memory_space=pl.ANY)
    vmem = pl.BlockSpec(memory_space=pltpu.VMEM)
    dma = pltpu.SemaphoreType.DMA
    small = (queries, hidden_in, norm_gain, route_logits, expert_ids, new_kv)
    return pl.pallas_call(
        functools.partial(layer_kernel, n),
        out_shape=(
            pltpu.VMEM((tokens, width), bf16),
            pltpu.VMEM(kv_cache.shape, bf16),
        ),
        in_specs=[hbm] * 11,
        out_specs=(vmem, vmem),
        scratch_shapes=[pltpu.VMEM(a.shape, a.dtype) for a in small]
        + [
            pltpu.SMEM(cycle_pos.shape, cycle_pos.dtype),
            pltpu.VMEM((2,) + out_weight.shape, bf16),
            pltpu.VMEM((2,) + expert_in.shape[1:], bf16),
            pltpu.VMEM((2,) + expert_out.shape[1:], bf16),
            pltpu.VMEM((heads_all * tokens, HD), f32),
            pltpu.VMEM((heads_all * tokens, slots), f32),
            pltpu.VMEM((heads_all * tokens, HD), f32),
            pltpu.VMEM(exchange, bf16),
            pltpu.VMEM(exchange, bf16),
            *[pltpu.VMEM((c, chips, tokens, p), bf16) for c, p in both],
            *[pltpu.VMEM((c, chips, tokens, p), bf16) for c, p in both],
            pltpu.VMEM((tokens, width), f32),
            pltpu.VMEM((CHUNKS[0] - 1, chips, tokens, part), bf16),
            pltpu.VMEM((chips, tokens, part + pad), bf16),
            pltpu.VMEM((2, chips * tokens, 2 * ff), f32),
            pltpu.VMEM((chips * tokens, 2 * ff), bf16),
            dma((11,)),
            dma((2 * CHUNKS[0] + PIECES[1],)),
            dma((2 * CHUNKS[0] + PIECES[1],)),
            dma,
            dma,
            *[dma((c,)) for c in CHUNKS],
            *[dma((c,)) for c in CHUNKS],
            dma((CHUNKS[0],)),
            dma((CHUNKS[0],)),
            *[pltpu.VMEM((c, chips // 2, tokens, p), bf16) for c, p in both],
            *[pltpu.VMEM((c, tokens, p), bf16) for c, p in both],
            *[dma((c, p)) for c, p in zip(CHUNKS, PIECES)],
            dma((CHUNKS[0],)),
        ],
        compiler_params=pltpu.CompilerParams(
            collective_id=0, has_side_effects=True, vmem_limit_bytes=56 * 1024 * 1024
        ),
        name="layer",
    )(
        queries,
        hidden_in,
        norm_gain,
        route_logits,
        expert_ids,
        new_kv,
        cycle_pos,
        kv_cache,
        out_weight,
        expert_in,
        expert_out,
    )


def store_kernel(hidden, cache, hidden_out, new_cache, sems):
    copies = (
        pltpu.make_async_copy(cache, new_cache, sems.at[1]),
        pltpu.make_async_copy(hidden, hidden_out, sems.at[0]),
    )
    for copy in copies:
        copy.start()
    for copy in copies:
        copy.wait()


def store(hidden, cache):
    anywhere = pl.BlockSpec(memory_space=pl.ANY)
    return pl.pallas_call(
        store_kernel,
        out_shape=tuple(jax.ShapeDtypeStruct(a.shape, a.dtype) for a in (hidden, cache)),
        in_specs=[pl.BlockSpec(memory_space=pltpu.VMEM)] * 2,
        out_specs=(anywhere,) * 2,
        scratch_shapes=[pltpu.SemaphoreType.DMA((2,))],
        name="store",
    )(*(pltpu.with_memory_space_constraint(a, pltpu.VMEM) for a in (hidden, cache)))


def on_device(
    hidden_in,
    queries,
    kv_cache,
    new_kv,
    cycle_pos,
    out_weight,
    norm_gain,
    route_logits,
    expert_ids,
    expert_in,
    expert_out,
):
    devices = lax.axis_size("tensor")
    hidden, cache = layer(
        devices,
        queries,
        hidden_in,
        norm_gain.reshape(1, -1),
        route_logits,
        expert_ids,
        new_kv,
        cycle_pos,
        kv_cache,
        (out_weight, expert_in, expert_out),
    )
    return store(hidden, cache)


def solution(mesh):
    return jax.shard_map(
        on_device,
        mesh=mesh,
        in_specs=(
            P(("group", "tensor"), None),
            P(("group", "tensor"), None),
            P(("group", "tensor"), None, None),
            P(("group", "tensor"), None),
            P("group"),
            P("tensor", None),
            P(),
            P(("group", "tensor"), None),
            P(("group", "tensor"), None),
            P("tensor", None, None),
            P("tensor", None, None),
        ),
        out_specs=(P(("group", "tensor"), None), P(("group", "tensor"), None, None)),
        check_vma=False,
    )
```
